512 devices in a mesh: sec: 4 (over y_hi), gx: 16 (over z, core), gy: 8 (over y_lo, x).
Axes of the slice: x: 4, y: 8 (y_hi: 4, y_lo: 2; y = y_hi * 2 + y_lo), z: 8, core: 2. Of those that a mesh axis runs over, the one named last changes fastest.
Arguments:
- composition_matrix: float32 [22, 128, 128, 512], P(None, 'gx', 'gy', 'sec'), may hold values from 0 to 1
- local_mixing_coefficient: float32 [128, 128, 512], P('gx', 'gy', 'sec'), may hold values from 0.3 to 3
- thermal_field: float32 [128, 128, 512], P('gx', 'gy', 'sec'), may hold values from 0.5 to 2
- component_mixing_weight: float32 [22], replicated, may hold values from 0.05 to 1
- kinetics_jacobian: float32 [22, 22], replicated, may hold values from -1.25 to 1.25
- mixture_classes: int32 [128, 128, 512], P('gx', 'gy', 'sec'), may hold values from 0 to 63, as said below
- streamwise_positions: int32 [128], replicated, may hold values from 0 to 63, as said below
Outputs:
- advanced_composition: float32 [22, 128, 128, 512], P(None, 'gx', 'gy', 'sec')
- cond_means: float32 [22, 64, 64], P(None, 'gx')
The draws below stay inside these ranges and needn't reach their ends.
Inputs may be any that keep to these rules, and one draw needn't show every extreme that they name: `mixture_classes`: bins of each plane cluster around a plane-dependent range. `streamwise_positions`: plane p has station ((p + h) // 2) mod 64 for one odd h between 1 and 7, so each station holds two axial planes.
All inputs are finite; a program needn't handle non-finite values.
Results may differ from the reference program's by a relative error of at most 0.0003.
Values sent between devices are 32-bit elements; how exact they have to be, the bound alone decides.
A program may use at most 64 MiB of HBM per device.

```python
import math
import jax
import jax.numpy as jnp
from jax import lax

S = 22
NB = 64
CX = 8
STREAMWISE_SLABS = 128
LATERAL_VOXELS = 128
SPANWISE_VOXELS = 512
NST = 64


def draw_mixture_classes(key, part):
    key_low = jax.random.fold_in(key, 11)
    key_noise = jax.random.fold_in(key, 12)
    plane = jnp.arange(STREAMWISE_SLABS, dtype=jnp.int32)
    lowest = jax.random.randint(key_low, (STREAMWISE_SLABS,), 0, 33, dtype=jnp.int32)
    lowest = jnp.where(plane == 0, 0, jnp.where(plane == STREAMWISE_SLABS - 1, 32, lowest))
    across = jnp.arange(LATERAL_VOXELS, dtype=jnp.int32) * 32 // LATERAL_VOXELS
    noise = jax.random.randint(key_noise, (STREAMWISE_SLABS, LATERAL_VOXELS, SPANWISE_VOXELS), -4, 5, dtype=jnp.int32)
    result = lowest[:, None, None] + across[None, :, None] + noise
    return jnp.clip(result, 0, NB - 1).astype(jnp.int32)


def draw_streamwise_positions(key, part):
    key_shift = jax.random.fold_in(key, 21)
    shift = 2 * jax.random.randint(key_shift, (), 0, CX // 2, dtype=jnp.int32) + 1
    plane = jnp.arange(STREAMWISE_SLABS, dtype=jnp.int32)
    return ((plane + shift) // 2 % NST).astype(jnp.int32)


def steps_of(key, extent, split, least, largest):
    loudness, own = 1.0, jax.random.fold_in(key, 6)
    for dim, shards_of in split:
        heights = jnp.exp(jax.random.uniform(jax.random.fold_in(own, dim), (shards_of,), jnp.float32, least / len(split), largest / len(split)))
        loudness = loudness * jnp.repeat(heights, extent[dim] // shards_of).reshape([-1 if axis == dim else 1 for axis in range(len(extent))])
    return loudness


def gaussian(own_key, extent, spread, reach, kind=jnp.bfloat16):
    values = spread * jax.random.normal(own_key, extent, jnp.float32)
    return jnp.clip(values, min=-reach, max=reach).astype(kind)


def setup_inputs(seed: int = 0) -> dict:
    seeds = jax.random.split(jax.random.key(seed), 8)
    return {
        "composition_matrix": jnp.clip(1.0 * jax.random.uniform(seeds[0], (S, STREAMWISE_SLABS, LATERAL_VOXELS, SPANWISE_VOXELS), jnp.float32) ** steps_of(seeds[0], (S, STREAMWISE_SLABS, LATERAL_VOXELS, SPANWISE_VOXELS), ((1, 16), (2, 8), (3, 4)), -0.2, 0.2), 0.0, 1.0),
        "local_mixing_coefficient": jnp.clip(jnp.exp(math.log(3.0) - 2.3025851 * jax.random.uniform(seeds[1], (STREAMWISE_SLABS, LATERAL_VOXELS, SPANWISE_VOXELS), jnp.float32) ** steps_of(seeds[1], (STREAMWISE_SLABS, LATERAL_VOXELS, SPANWISE_VOXELS), ((0, 16), (1, 8), (2, 4)), -0.2, 0.2)), 0.3, 3.0),
        "thermal_field": jnp.clip(0.5 + 1.5 * jax.random.uniform(seeds[2], (STREAMWISE_SLABS, LATERAL_VOXELS, SPANWISE_VOXELS), jnp.float32) ** steps_of(seeds[2], (STREAMWISE_SLABS, LATERAL_VOXELS, SPANWISE_VOXELS), ((0, 16), (1, 8), (2, 4)), -0.2, 0.2), 0.5, 2.0),
        "component_mixing_weight": jnp.clip(jnp.exp(jax.random.uniform(seeds[3], (S,), jnp.float32, math.log(0.05), math.log(1.0))), 0.05, 1.0),
        "kinetics_jacobian": gaussian(seeds[4], (S, S), S ** -0.5, 1.25, jnp.float32),
        "mixture_classes": draw_mixture_classes(jax.random.fold_in(seeds[7], 71), 0),
        "streamwise_positions": draw_streamwise_positions(jax.random.fold_in(seeds[7], 71), 0),
    }


def neighbour(padded_composition, axis, start):
    index = [slice(None), slice(1, -1), slice(1, -1), slice(1, -1)]
    index[axis] = slice(start, start + padded_composition.shape[axis] - 2)
    return padded_composition[tuple(index)]


def advance_explicit_step(padded_composition, interior_block, thermal_field, component_mixing_weight, kinetics_jacobian):
    central_voxels = interior_block[:-1]
    diff_core = interior_block[-1]
    total = jnp.zeros_like(central_voxels)
    for axis in (1, 2, 3):
        for start in (0, 2):
            other = neighbour(padded_composition, axis, start)
            total = total + 0.5 * (diff_core + other[-1]) * (other[:-1] - central_voxels)
    averaged_composition = jnp.einsum("kj,jxyz->kxyz", kinetics_jacobian, central_voxels, precision=lax.Precision.HIGHEST)
    reactive_yield_term = 4.0 * jnp.exp(-2.0 / thermal_field) * averaged_composition
    return central_voxels + 0.05 * (component_mixing_weight[:, None, None, None] * total + reactive_yield_term)


def reference(composition_matrix, local_mixing_coefficient, thermal_field, component_mixing_weight, kinetics_jacobian, mixture_classes, streamwise_positions):
    collected_slabs = jnp.concatenate([composition_matrix, local_mixing_coefficient[None]], axis=0)
    padded_composition = jnp.pad(collected_slabs, ((0, 0), (1, 1), (1, 1), (1, 1)))
    advanced_composition = advance_explicit_step(padded_composition, collected_slabs, thermal_field, component_mixing_weight, kinetics_jacobian)
    values = jnp.concatenate([advanced_composition, jnp.ones_like(advanced_composition[:1])], axis=0)
    levels = jnp.arange(NB, dtype=jnp.int32)

    def plane_sums(item):
        plane, plane_bins = item
        onehot = (plane_bins[None] == levels[:, None, None]).astype(jnp.float32)
        return jnp.einsum("kyz,byz->kb", plane, onehot, precision=lax.Precision.HIGHEST)

    partial_sums = lax.map(plane_sums, (jnp.moveaxis(values, 1, 0), mixture_classes))
    owner = (streamwise_positions[:, None] == jnp.arange(NST, dtype=jnp.int32)[None]).astype(jnp.float32)
    totals = jnp.einsum("xkb,xs->ksb", partial_sums, owner, precision=lax.Precision.HIGHEST)
    cond_means = totals[:-1] / jnp.maximum(totals[-1], 1.0)[None]
    return advanced_composition, cond_means
```

```python
import functools

import jax
import jax.numpy as jnp
from jax import lax
from jax.experimental import pallas as pl
from jax.experimental.pallas import tpu as pltpu
from jax.sharding import PartitionSpec as P

NB = 64
YLO = 2
F32, BF16 = jnp.float32, jnp.bfloat16
MESH = pl.DeviceIdType.MESH
GROUPS = ((0,), (1, 2), (3, 4), (5, 6), (7,))


def kernel(
    species,
    comp_hbm,
    diff_hbm,
    temp_hbm,
    weight_hbm,
    jac_hbm,
    bins_hbm,
    pos_hbm,
    adv_hbm,
    cond_ref,
    u,
    adv,
    onehot,
    onehot_z,
    rate,
    temp,
    bins,
    jac,
    jac_pad,
    weight,
    pos,
    psum,
    zsend,
    zrecv,
    nxt,
    r1a,
    r1b,
    r2a,
    r2b,
    in_sem,
    out_sem,
    hs_sem,
    hr_sem,
    s1a,
    q1a,
    s1b,
    q1b,
    s2a,
    q2a,
    s2b,
    q2b,
):
    nsec, ngx, ngy = lax.axis_size("sec"), lax.axis_size("gx"), lax.axis_size("gy")
    nx, ny = ngy // YLO, nsec * YLO
    sec, gx, gy = lax.axis_index("sec"), lax.axis_index("gx"), lax.axis_index("gy")
    my_x, my_y = lax.rem(gy, nx), sec * YLO + gy // nx
    planes, rows = 8, 16
    dummy = species

    def device(s, i, g):
        return {"sec": s, "gx": i, "gy": g}

    def at_xy(i, x, y):
        return device(y // YLO, i, lax.rem(y, YLO) * nx + x)

    right, left = lax.rem(gx + 1, ngx), lax.rem(gx + ngx - 1, ngx)
    front, back = lax.rem(gy + 1, ngy), lax.rem(gy + ngy - 1, ngy)
    up, down = lax.rem(sec + 1, nsec), lax.rem(sec + nsec - 1, nsec)

    loads = [
        pltpu.make_async_copy(comp_hbm.at[s], u.at[1:9, 1:17, s, :], in_sem.at[s])
        for s in range(species)
    ]
    loads += [
        pltpu.make_async_copy(diff_hbm, u.at[1:9, 1:17, species + r, :], in_sem.at[species + r])
        for r in range(2)
    ]
    first = [
        pltpu.make_async_copy(bins_hbm, bins, in_sem.at[24]),
        pltpu.make_async_copy(temp_hbm, temp, in_sem.at[25]),
        pltpu.make_async_copy(jac_hbm, jac, in_sem.at[26]),
        pltpu.make_async_copy(weight_hbm, weight, in_sem.at[27]),
        pltpu.make_async_copy(pos_hbm, pos, in_sem.at[28]),
    ]
    for copy in first + loads:
        copy.start()

    barrier = pltpu.get_barrier_semaphore()
    peers = [device(sec, gx, front), device(sec, gx, back)]
    peers += [at_xy(gx, lax.rem(my_x + o, nx), my_y) for o in range(1, nx)]
    peers += [at_xy(gx, my_x, lax.rem(my_y + o, ny)) for o in range(1, ny)]
    for side in (right, left):
        peers += [at_xy(side, lax.rem(my_x + o, nx), my_y) for o in range(nx)]
        peers += [at_xy(side, my_x, lax.rem(my_y + o, ny)) for o in range(1, ny)]
    for peer in peers:
        pl.semaphore_signal(barrier, inc=1, device_id=peer, device_id_type=MESH)

    for copy in first:
        copy.wait()
    level = lax.broadcasted_iota(jnp.int32, (NB, 128), 0)

    def prepare(x, carry):
        for y in range(rows):
            row = bins[x, pl.ds(y, 1), :]
            onehot[x, :, y * 128 : (y + 1) * 128] = jnp.where(
                jnp.broadcast_to(row, (NB, 128)) == level, 1.0, 0.0
            ).astype(BF16)
        rate[x] = 0.2 * jnp.exp(-2.0 / temp[x])
        return carry

    lax.fori_loop(0, planes, prepare, 0)
    across = jnp.transpose(bins[...].reshape(planes * rows, 128).astype(F32))
    lane1 = lax.broadcasted_iota(jnp.int32, (1, 128), 1)
    group_of = (lane1 // rows + 1) // 2
    code_level = lax.broadcasted_iota(jnp.int32, (5 * NB, 128), 0)
    for side, lane in ((0, 0), (1, 127)):
        code = across[lane : lane + 1, :].astype(jnp.int32) + group_of * NB
        onehot_z[side] = jnp.where(
            jnp.broadcast_to(code, (5 * NB, 128)) == code_level, 1.0, 0.0
        ).astype(BF16)

    jac_pad[...] = jnp.zeros_like(jac_pad)
    jac_pad[0:species, 0:species] = jac[...]
    j_full = jac_pad[...]
    j_hi = j_full.astype(BF16)
    j_lo = (j_full - j_hi.astype(F32)).astype(BF16)
    row_id = lax.broadcasted_iota(jnp.int32, (24, 128), 0)
    lane_id = lax.broadcasted_iota(jnp.int32, (24, 128), 1)
    wk = jnp.zeros((24, 128), F32)
    for s in range(species):
        wk = jnp.where(row_id == s, 0.05 * weight[s], wk)

    for copy in loads:
        copy.wait()

    def pack(x, carry):
        low, high = carry
        for y in range(rows):
            j = x * rows + y
            turned = pltpu.roll(u[x + 1, y + 1], j, 1)
            low = jnp.where(lane_id == j, turned, low)
            high = jnp.where(lane_id == lax.rem(j + 127, 128), turned, high)
        return low, high

    blank = jnp.zeros((24, 128), F32)
    low, high = lax.fori_loop(0, planes, pack, (blank, blank))
    zsend[0] = low
    zsend[1] = pltpu.roll(high, 1, 1)

    pl.semaphore_wait(barrier, len(peers))

    def remote(src, dst, send, recv, peer):
        return pltpu.make_async_remote_copy(
            src_ref=src, dst_ref=dst, send_sem=send, recv_sem=recv, device_id=peer,
            device_id_type=MESH,
        )

    halo = [
        remote(u.at[8, 1:17], u.at[0, 1:17], hs_sem.at[0], hr_sem.at[0], device(sec, right, gy)),
        remote(u.at[1, 1:17], u.at[9, 1:17], hs_sem.at[1], hr_sem.at[1], device(sec, left, gy)),
        remote(u.at[1:9, 16], u.at[1:9, 0], hs_sem.at[2], hr_sem.at[2], device(sec, gx, front)),
        remote(u.at[1:9, 1], u.at[1:9, 17], hs_sem.at[3], hr_sem.at[3], device(sec, gx, back)),
        remote(zsend.at[1], zrecv.at[0], hs_sem.at[4], hr_sem.at[4], device(up, gx, gy)),
        remote(zsend.at[0], zrecv.at[1], hs_sem.at[5], hr_sem.at[5], device(down, gx, gy)),
    ]
    for copy in halo:
        copy.start()

    def dot(a, b):
        return lax.dot_general(a, b, (((1,), (0,)), ((), ())), preferred_element_type=F32)

    def dot_t(a, b):
        return lax.dot_general(a, b, (((1,), (1,)), ((), ())), preferred_element_type=F32)

    def binned(values, hot):
        hi = values.astype(BF16)
        lo = (values - hi.astype(F32)).astype(BF16)
        return dot_t(hi, hot) + dot_t(lo, hot)

    not_last, not_first = lane1 < 127, lane1 > 0

    def inner(x, carry):
        whole = jnp.concatenate([u[x + 1, y + 1] for y in range(rows)], axis=1)
        hi = whole.astype(BF16)
        lo = (whole - hi.astype(F32)).astype(BF16)
        source = dot(j_hi, hi) + dot(j_hi, lo) + dot(j_lo, hi)
        done = []
        xm, xp = jnp.maximum(x, 1), jnp.minimum(x + 2, 8)
        for y in range(rows):
            c = u[x + 1, y + 1]
            d = c[dummy : dummy + 1]
            flux = None
            for other in (
                u[xm, y + 1],
                u[xp, y + 1],
                u[x + 1, max(y, 1)],
                u[x + 1, min(y + 2, 16)],
            ):
                term = (0.5 * (d + other[dummy : dummy + 1])) * (other - c)
                flux = term if flux is None else flux + term
            for turn, keep in ((127, not_last), (1, not_first)):
                other = pltpu.roll(c, turn, 1)
                half = jnp.where(keep, 0.5 * (d + other[dummy : dummy + 1]), 0.0)
                flux = flux + half * (other - c)
            part = source[:, y * 128 : (y + 1) * 128]
            value = c + wk * flux + rate[x, pl.ds(y, 1), :] * part
            adv[x, y] = value
            done.append(jnp.where(row_id == dummy, 1.0, value))
        psum[x] = binned(jnp.concatenate(done, axis=1), onehot[x])
        return carry

    lax.fori_loop(0, planes, inner, 0)

    for copy in halo:
        copy.wait()

    def face(c, other, inside):
        gate = jnp.where(inside, 1.0, 0.0)
        other = other * gate
        return wk * (0.5 * (c[dummy : dummy + 1] + other[dummy : dummy + 1]) * (other - c))

    for x, ghost, inside in ((0, 0, gx > 0), (7, 9, gx < ngx - 1)):
        terms = []
        for y in range(rows):
            term = face(u[x + 1, y + 1], u[ghost, y + 1], inside)
            adv[x, y] = adv[x, y] + term
            terms.append(term)
        psum[x] = psum[x] + binned(jnp.concatenate(terms, axis=1), onehot[x])

    def faces_y(x, carry):
        total = psum[x]
        for y, ghost, inside in ((0, 0, gy > 0), (15, 17, gy < ngy - 1)):
            term = face(u[x + 1, y + 1], u[x + 1, ghost], inside)
            adv[x, y] = adv[x, y] + term
            total = total + binned(term, onehot[x, :, y * 128 : (y + 1) * 128])
        psum[x] = total
        return carry

    lax.fori_loop(0, planes, faces_y, 0)
    ends = [
        face(zsend[0], zrecv[0], sec > 0),
        face(zsend[1], zrecv[1], sec < nsec - 1),
    ]
    by_group = binned(ends[0], onehot_z[0]) + binned(ends[1], onehot_z[1])

    count = pos.shape[0] // 2
    per = count // ngx
    sums = []
    for g, members in enumerate(GROUPS):
        total = by_group[:, g * NB : (g + 1) * NB]
        for x in members:
            total = total + psum[x]
        sums.append((pos[gx * planes + members[0]], total))

    def table(slot):
        target = lax.rem(gx * per + slot, count)
        out = jnp.zeros((24, NB), F32)
        for station, total in sums:
            out = out + jnp.where(station == target, 1.0, 0.0) * total
        return out

    slots = [table(s) for s in range(2 * per)]
    r1a[0, my_x] = jnp.concatenate(slots[0:2], axis=1)
    r1b[0, my_y] = jnp.concatenate(slots[2:4], axis=1)
    nxt[0] = jnp.concatenate(slots[4:6], axis=1)
    nxt[1] = jnp.concatenate(slots[6:8], axis=1)

    waits = []
    for o in range(ny):
        y = lax.rem(my_y + o, ny)
        if o:
            c = remote(r1b.at[0, my_y], r1b.at[0, my_y], s1b.at[0, o], q1b.at[0, my_y], at_xy(gx, my_x, y))
            c.start()
            waits.append(c)
        c = remote(nxt.at[1], r1b.at[1, my_y], s1b.at[1, o], q1b.at[1, my_y], at_xy(right, my_x, y))
        c.start()
        waits.append(c)
    for o in range(nx):
        x = lax.rem(my_x + o, nx)
        if o:
            c = remote(r1a.at[0, my_x], r1a.at[0, my_x], s1a.at[0, o], q1a.at[0, my_x], at_xy(gx, x, my_y))
            c.start()
            waits.append(c)
        c = remote(nxt.at[0], r1a.at[1, my_x], s1a.at[1, o], q1a.at[1, my_x], at_xy(right, x, my_y))
        c.start()
        waits.append(c)

    def ends_in(x, carry):
        a, b = carry
        for y in range(rows):
            j = x * rows + y
            head = pltpu.roll(a, lax.rem(128 - j, 128), 1)
            tail = pltpu.roll(b, lax.rem(255 - j, 128), 1)
            adv[x, y] = adv[x, y] + jnp.where(
                lane_id == 0, head, jnp.where(lane_id == 127, tail, 0.0)
            )
        return carry

    lax.fori_loop(0, planes, ends_in, (ends[0], ends[1]))
    outs = [
        pltpu.make_async_copy(adv.at[:, :, s, :], adv_hbm.at[s], out_sem.at[s])
        for s in range(species)
    ]
    for copy in outs:
        copy.start()

    def arrived(buffer, sem):
        pltpu.make_async_copy(buffer, buffer, sem).wait()

    def gather(buffer, sems, mine, size, layers):
        for o in range(size):
            slot = lax.rem(mine + o, size)
            for layer in range(layers):
                if layer or o:
                    arrived(buffer.at[layer, slot], sems.at[layer, slot])
        total = buffer[0, 0]
        for layer in range(layers):
            for slot in range(size):
                if layer or slot:
                    total = total + buffer[layer, slot]
        return total

    r2a[0, my_y] = gather(r1a, q1a, my_x, nx, 2)
    for o in range(1, ny):
        y = lax.rem(my_y + o, ny)
        c = remote(r2a.at[0, my_y], r2a.at[0, my_y], s2a.at[0, o], q2a.at[0, my_y], at_xy(gx, my_x, y))
        c.start()
        waits.append(c)
    r2b[0, my_x] = gather(r1b, q1b, my_y, ny, 2)
    for o in range(1, nx):
        x = lax.rem(my_x + o, nx)
        c = remote(r2b.at[0, my_x], r2b.at[0, my_x], s2b.at[0, o], q2b.at[0, my_x], at_xy(gx, x, my_y))
        c.start()
        waits.append(c)
    halves = [gather(r2a, q2a, my_y, ny, 1), gather(r2b, q2b, my_x, nx, 1)]
    for half in range(2):
        whole = halves[half]
        means = whole / jnp.maximum(whole[dummy : dummy + 1], 1.0)
        for part in range(2):
            cond_ref[:, 2 * half + part, :] = means[0:species, part * NB : (part + 1) * NB]
    for copy in waits:
        copy.wait_send()
    for copy in outs:
        copy.wait()


def on_device(comp, diff, temp, weight, jac, bins, pos):
    species, planes, rows, cells = comp.shape
    nx = lax.axis_size("gy") // YLO
    ny = lax.axis_size("sec") * YLO
    per = pos.shape[0] // 2 // lax.axis_size("gx")
    dma = pltpu.SemaphoreType.DMA
    anywhere = pl.BlockSpec(memory_space=pl.ANY)
    return pl.pallas_call(
        functools.partial(kernel, species),
        out_shape=(
            jax.ShapeDtypeStruct(comp.shape, F32),
            jax.ShapeDtypeStruct((species, per, NB), F32),
        ),
        in_specs=[anywhere] * 7,
        out_specs=(anywhere, pl.BlockSpec(memory_space=pltpu.VMEM)),
        scratch_shapes=[
            pltpu.VMEM((planes + 2, rows + 2, 24, cells), F32),
            pltpu.VMEM((planes, rows, 24, cells), F32),
            pltpu.VMEM((planes, NB, rows * cells), BF16),
            pltpu.VMEM((2, 5 * NB, cells), BF16),
            pltpu.VMEM((planes, rows, cells), F32),
            pltpu.VMEM((planes, rows, cells), F32),
            pltpu.VMEM((planes, rows, cells), jnp.int32),
            pltpu.VMEM(jac.shape, F32),
            pltpu.VMEM((24, 24), F32),
            pltpu.SMEM(weight.shape, F32),
            pltpu.SMEM(pos.shape, jnp.int32),
            pltpu.VMEM((planes, 24, NB), F32),
            pltpu.VMEM((2, 24, cells), F32),
            pltpu.VMEM((2, 24, cells), F32),
            pltpu.VMEM((2, 24, 2 * NB), F32),
            pltpu.VMEM((2, nx, 24, 2 * NB), F32),
            pltpu.VMEM((2, ny, 24, 2 * NB), F32),
            pltpu.VMEM((1, ny, 24, 2 * NB), F32),
            pltpu.VMEM((1, nx, 24, 2 * NB), F32),
            dma((29,)),
            dma((species,)),
            dma((6,)),
            dma((6,)),
            dma((2, nx)),
            dma((2, nx)),
            dma((2, ny)),
            dma((2, ny)),
            dma((1, ny)),
            dma((1, ny)),
            dma((1, nx)),
            dma((1, nx)),
        ],
        compiler_params=pltpu.CompilerParams(collective_id=0, has_side_effects=True),
        name="section",
    )(comp, diff, temp, weight, jac, bins, pos)


def solution(mesh):
    in_specs = (
        P(None, "gx", "gy", "sec"),
        P("gx", "gy", "sec"),
        P("gx", "gy", "sec"),
        P(),
        P(),
        P("gx", "gy", "sec"),
        P(),
    )
    out_specs = (P(None, "gx", "gy", "sec"), P(None, "gx", None))
    return jax.shard_map(
        on_device, mesh=mesh, in_specs=in_specs, out_specs=out_specs, check_vma=False
    )
```

```python
import functools

import jax
import jax.numpy as jnp
from jax import lax
from jax.experimental import pallas as pl
from jax.experimental.pallas import tpu as pltpu
from jax.sharding import PartitionSpec as P

NB = 64
YLO = 2
ROWS = 24
F32, BF16 = jnp.float32, jnp.bfloat16
MESH = pl.DeviceIdType.MESH
GROUPS = ((0,), (1, 2), (3, 4), (5, 6), (7,))


def remote(src, dst, send, recv, peer):
    return pltpu.make_async_remote_copy(
        src_ref=src, dst_ref=dst, send_sem=send, recv_sem=recv, device_id=peer, device_id_type=MESH
    )


def split(values):
    hi = values.astype(BF16).astype(F32)
    return jnp.concatenate([hi, values - hi], axis=0).astype(BF16)


def binned(values, hot):
    both = lax.dot_general(
        split(values), hot, (((1,), (1,)), ((), ())), preferred_element_type=F32
    )
    return both[0:ROWS] + both[ROWS : 2 * ROWS]


def kernel(
    species,
    comp_hbm,
    diff_hbm,
    temp_hbm,
    weight_hbm,
    jac_hbm,
    bins_hbm,
    pos_hbm,
    adv,
    sums,
    u,
    onehot,
    onehot_z,
    rate,
    flux_x,
    temp,
    bins,
    jac,
    jac_pad,
    weight,
    pos,
    psum,
    zsend,
    zrecv,
    r1a,
    r1b,
    next_a,
    next_b,
    r2a,
    r2b,
    in_sem,
    hs_sem,
    hr_sem,
    s1a,
    q1a,
    s1b,
    q1b,
    s2a,
    q2a,
    s2b,
    q2b,
    ready,
):
    nsec, ngx, ngy = lax.axis_size("sec"), lax.axis_size("gx"), lax.axis_size("gy")
    nx, ny = ngy // YLO, nsec * YLO
    sec, gx, gy = lax.axis_index("sec"), lax.axis_index("gx"), lax.axis_index("gy")
    my_x, my_y = lax.rem(gy, nx), sec * YLO + gy // nx
    planes, rows = 8, 16
    dif = species

    def device(s, i, g):
        return {"sec": s, "gx": i, "gy": g}

    def at_xy(i, x, y):
        return device(y // YLO, i, lax.rem(y, YLO) * nx + x)

    right, left = lax.rem(gx + 1, ngx), lax.rem(gx + ngx - 1, ngx)
    front, back = lax.rem(gy + 1, ngy), lax.rem(gy + ngy - 1, ngy)
    up, down = lax.rem(sec + 1, nsec), lax.rem(sec + nsec - 1, nsec)

    loads = [
        pltpu.make_async_copy(comp_hbm.at[s], u.at[1:9, 1:17, s, :], in_sem.at[s])
        for s in range(species)
    ]
    loads.append(pltpu.make_async_copy(diff_hbm, u.at[1:9, 1:17, dif, :], in_sem.at[species]))
    first = [
        pltpu.make_async_copy(bins_hbm, bins, in_sem.at[24]),
        pltpu.make_async_copy(temp_hbm, temp, in_sem.at[25]),
        pltpu.make_async_copy(jac_hbm, jac, in_sem.at[26]),
        pltpu.make_async_copy(weight_hbm, weight, in_sem.at[27]),
        pltpu.make_async_copy(pos_hbm, pos, in_sem.at[28]),
    ]
    for copy in loads:
        copy.start()

    barrier = pltpu.get_barrier_semaphore()
    peers = [
        device(sec, right, gy),
        device(sec, left, gy),
        device(sec, gx, front),
        device(sec, gx, back),
        device(up, gx, gy),
        device(down, gx, gy),
        at_xy(gx, lax.rem(my_x + 1, nx), my_y),
        at_xy(gx, lax.rem(my_x + nx - 1, nx), my_y),
        at_xy(gx, my_x, lax.rem(my_y + 1, ny)),
        at_xy(gx, my_x, lax.rem(my_y + ny - 1, ny)),
    ]
    for peer in peers:
        pl.semaphore_signal(barrier, inc=1, device_id=peer, device_id_type=MESH)
    for copy in first:
        copy.start()

    ones = jnp.ones((1, 128), F32)
    level = lax.broadcasted_iota(jnp.int32, (NB, 128), 0)
    for copy in first:
        copy.wait()

    def prepare(x, carry):
        for y in range(rows):
            row = bins[x, pl.ds(y, 1), :]
            onehot[x, :, y * 128 : (y + 1) * 128] = jnp.where(
                jnp.broadcast_to(row, (NB, 128)) == level, 1.0, 0.0
            ).astype(BF16)
            u[x + 1, y + 1, dif + 1 : dif + 2, :] = ones
        rate[x] = 0.2 * jnp.exp(-2.0 / temp[x])
        return carry

    lax.fori_loop(0, planes, prepare, 0)
    flux_x[...] = jnp.zeros_like(flux_x)
    jac_pad[...] = jnp.zeros_like(jac_pad)
    jac_pad[0:species, 0:species] = jac[...]
    j_full = jac_pad[...]
    j_hi = j_full.astype(BF16).astype(F32)
    j_lo = j_full - j_hi
    j_all = jnp.concatenate([j_hi, j_hi, j_lo, j_lo], axis=1).astype(BF16)
    row_id = lax.broadcasted_iota(jnp.int32, (ROWS, 128), 0)
    lane_id = lax.broadcasted_iota(jnp.int32, (ROWS, 128), 1)
    wk = jnp.zeros((ROWS, 128), F32)
    for s in range(species):
        wk = jnp.where(row_id == s, 0.025 * weight[s], wk)

    for copy in loads:
        copy.wait()
    pl.semaphore_wait(barrier, len(peers))
    halo = [
        remote(u.at[8, 1:17], u.at[0, 1:17], hs_sem.at[0], hr_sem.at[0], device(sec, right, gy)),
        remote(u.at[1, 1:17], u.at[9, 1:17], hs_sem.at[1], hr_sem.at[1], device(sec, left, gy)),
        remote(u.at[1:9, 16], u.at[1:9, 0], hs_sem.at[2], hr_sem.at[2], device(sec, gx, front)),
        remote(u.at[1:9, 1], u.at[1:9, 17], hs_sem.at[3], hr_sem.at[3], device(sec, gx, back)),
        remote(zsend.at[1], zrecv.at[0], hs_sem.at[4], hr_sem.at[4], device(up, gx, gy)),
        remote(zsend.at[0], zrecv.at[1], hs_sem.at[5], hr_sem.at[5], device(down, gx, gy)),
    ]
    for copy in halo[0:4]:
        copy.start()

    def pack(x, carry):
        low, high = carry
        heads = tails = None
        for y in range(rows):
            c = u[x + 1, y + 1]
            turned = pltpu.roll(c, y, 1) if y else c
            heads = turned if y == 0 else jnp.where(lane_id == y, turned, heads)
            tails = turned if y == 0 else jnp.where(lane_id == y - 1, turned, tails)
        here = lane_id // rows == x
        low = jnp.where(here, pltpu.roll(heads, x * rows, 1), low)
        high = jnp.where(here, pltpu.roll(tails, x * rows + 1, 1), high)
        return low, high

    blank = jnp.zeros((ROWS, 128), F32)
    low, high = lax.fori_loop(0, planes, pack, (blank, blank))
    zsend[0] = low
    zsend[1] = high
    for copy in halo[4:6]:
        copy.start()

    across = jnp.transpose(bins[...].reshape(planes * rows, 128).astype(F32))
    lane1 = lax.broadcasted_iota(jnp.int32, (1, 128), 1)
    group_of = (lane1 // rows + 1) // 2
    code_level = lax.broadcasted_iota(jnp.int32, (5 * NB, 128), 0)
    for side, lane in ((0, 0), (1, 127)):
        code = across[lane : lane + 1, :].astype(jnp.int32) + group_of * NB
        onehot_z[side] = jnp.where(
            jnp.broadcast_to(code, (5 * NB, 128)) == code_level, 1.0, 0.0
        ).astype(BF16)

    inside = lax.broadcasted_iota(jnp.int32, (1, 128), 1) < 127

    def inner(x, carry):
        parts = split(jnp.concatenate([u[x + 1, y + 1] for y in range(rows)], axis=1))
        source = jnp.dot(
            j_all, jnp.concatenate([parts, parts], axis=0), preferred_element_type=F32
        )
        done = []
        xp = jnp.minimum(x + 2, 8)
        flux_y = None
        for y in range(rows):
            c = u[x + 1, y + 1]
            d = u[x + 1, y + 1, dif : dif + 1, :]
            after = (d + u[xp, y + 1, dif : dif + 1, :]) * (u[xp, y + 1] - c)
            flux = after - flux_x[y]
            flux_x[y] = after
            if y < rows - 1:
                later = (d + u[x + 1, y + 2, dif : dif + 1, :]) * (u[x + 1, y + 2] - c)
                flux = flux + (later if flux_y is None else later - flux_y)
                flux_y = later
            else:
                flux = flux - flux_y
            turned = pltpu.roll(c, 127, 1)
            gain = jnp.where(inside, d + pltpu.roll(d, 127, 1), 0.0)
            out = gain * (turned - c)
            flux = flux + (out - pltpu.roll(out, 1, 1))
            part = source[:, y * 128 : (y + 1) * 128]
            value = (c + rate[x, pl.ds(y, 1), :] * part) + wk * flux
            adv[x, y] = value
            done.append(value)
        psum[x] = binned(jnp.concatenate(done, axis=1), onehot[x])
        return carry

    lax.fori_loop(0, planes, inner, 0)

    for copy in halo:
        copy.wait_recv()
    near = [at_xy(gx, lax.rem(my_x + o, nx), my_y) for o in range(1, nx)]
    near += [at_xy(gx, my_x, lax.rem(my_y + o, ny)) for o in range(1, ny)]
    for peer in near:
        pl.semaphore_signal(ready, inc=1, device_id=peer, device_id_type=MESH)

    def face(c, d, other, d_other, gate):
        return wk * ((d + d_other * gate) * (other * gate - c))

    def gate_of(there):
        return jnp.where(there, 1.0, 0.0)

    faces_x = []
    for x, ghost, gate in ((0, 0, gate_of(gx > 0)), (7, 9, gate_of(gx < ngx - 1))):
        terms = []
        for y in range(rows):
            term = face(
                u[x + 1, y + 1],
                u[x + 1, y + 1, dif : dif + 1, :],
                u[ghost, y + 1],
                u[ghost, y + 1, dif : dif + 1, :],
                gate,
            )
            adv[x, y] = adv[x, y] + term
            terms.append(term)
        faces_x.append(binned(jnp.concatenate(terms, axis=1), onehot[x]))

    gate_back, gate_front = gate_of(gy > 0), gate_of(gy < ngy - 1)
    plane_sums = []
    for x in range(planes):
        terms = []
        for y, ghost, gate in ((0, 0, gate_back), (15, 17, gate_front)):
            term = face(
                u[x + 1, y + 1],
                u[x + 1, y + 1, dif : dif + 1, :],
                u[x + 1, ghost],
                u[x + 1, ghost, dif : dif + 1, :],
                gate,
            )
            adv[x, y] = adv[x, y] + term
            terms.append(term)
        hot = jnp.concatenate([onehot[x, :, 0:128], onehot[x, :, 15 * 128 : 16 * 128]], axis=1)
        total = psum[x] + binned(jnp.concatenate(terms, axis=1), hot)
        if x in (0, 7):
            total = total + faces_x[x // 7]
        plane_sums.append(total)
    ends = []
    for side, gate in ((0, gate_of(sec > 0)), (1, gate_of(sec < nsec - 1))):
        c, other = zsend[side], zrecv[side]
        ends.append(face(c, c[dif : dif + 1], other, other[dif : dif + 1], gate))
    by_group = binned(ends[0], onehot_z[0]) + binned(ends[1], onehot_z[1])

    totals = []
    for g, members in enumerate(GROUPS):
        total = by_group[:, g * NB : (g + 1) * NB]
        for x in members:
            total = total + plane_sums[x]
        totals.append(total)
    totals.append(jnp.zeros_like(totals[0]))
    for k in range(3):
        pair = jnp.concatenate(totals[2 * k : 2 * k + 2], axis=1)
        r1b[0, my_y, :, k * 128 : (k + 1) * 128] = pair[8:24]
        r1a[0, my_x, :, k * 128 : (k + 1) * 128] = pair[0:8]

    waits = []

    def send(src, dst, sem, recv, peer):
        copy = remote(src, dst, sem, recv, peer)
        copy.start()
        waits.append(copy)

    far_y = sorted(range(1, ny), key=lambda o: -min(o, ny - o))
    far_x = sorted(range(1, nx), key=lambda o: -min(o, nx - o))
    for o in far_y:
        block = r1b.at[0, my_y]
        send(block, block, s1b.at[0, o], q1b.at[0, my_y], at_xy(gx, my_x, lax.rem(my_y + o, ny)))
    for o in far_x:
        block = r1a.at[0, my_x]
        send(block, block, s1a.at[0, o], q1a.at[0, my_x], at_xy(gx, lax.rem(my_x + o, nx), my_y))

    def ends_in(x, carry):
        a, b = carry
        a = pltpu.roll(a, lax.rem(128 - x * rows, 128), 1)
        b = pltpu.roll(b, 127 - x * rows, 1)
        for y in range(rows):
            head = pltpu.roll(a, 128 - y, 1) if y else a
            tail = pltpu.roll(b, 128 - y, 1) if y else b
            adv[x, y] = adv[x, y] + jnp.where(
                lane_id == 0, head, jnp.where(lane_id == 127, tail, 0.0)
            )
        return carry

    lax.fori_loop(0, planes, ends_in, (ends[0], ends[1]))

    def arrived(buffer, sem):
        pltpu.make_async_copy(buffer, buffer, sem).wait()

    def gather(buffer, sems, mine, size, layers):
        for o in range(size):
            slot = lax.rem(mine + o, size)
            for layer in range(layers):
                if layer or o:
                    arrived(buffer.at[layer, slot], sems.at[layer, slot])
        total = buffer[0, 0]
        for layer in range(layers):
            for slot in range(size):
                if layer or slot:
                    total = total + buffer[layer, slot]
        return total

    count = pos.shape[0] // 2
    per = count // ngx
    m = lax.rem(pos[gx * planes] - gx * per + count, count)

    def stations(total):
        p = [total[:, k * 128 : (k + 1) * 128] for k in range(3)]
        turned = [pltpu.roll(v, NB, 1) for v in p]
        high = lax.broadcasted_iota(jnp.int32, p[0].shape, 1) >= NB
        q = [jnp.where(high, turned[k], turned[k - 1] if k else 0.0) for k in range(3)]
        flag = [jnp.where(m == k, 1.0, 0.0) for k in range(4)]
        zero = jnp.zeros_like(p[0])
        shifted = (p + [zero], q + [zero], [zero] + p, [zero] + q)
        out = []
        for k in range(4):
            out.append(sum(flag[i] * shifted[i][k] for i in range(4)))
        return jnp.concatenate(out[0:2], axis=1), jnp.concatenate(out[2:4], axis=1)

    own, following = stations(gather(r1a, q1a, my_x, nx, 1))
    r2a[0, my_y] = own
    next_a[...] = following
    pl.semaphore_wait(ready, len(near))
    for o in far_y + [0]:
        peer = lax.rem(my_y + o, ny)
        send(next_a, r2a.at[1, my_y], s2a.at[1, o], q2a.at[1, my_y], at_xy(right, my_x, peer))
        if o:
            block = r2a.at[0, my_y]
            send(block, block, s2a.at[0, o], q2a.at[0, my_y], at_xy(gx, my_x, peer))
    own, following = stations(gather(r1b, q1b, my_y, ny, 1))
    r2b[0, my_x] = own
    next_b[...] = following
    for o in far_x + [0]:
        peer = lax.rem(my_x + o, nx)
        send(next_b, r2b.at[1, my_x], s2b.at[1, o], q2b.at[1, my_x], at_xy(right, peer, my_y))
        if o:
            block = r2b.at[0, my_x]
            send(block, block, s2b.at[0, o], q2b.at[0, my_x], at_xy(gx, peer, my_y))
    for copy in halo + waits:
        copy.wait_send()
    sums[8:24] = gather(r2b, q2b, my_x, nx, 2)
    sums[0:8] = gather(r2a, q2a, my_y, ny, 2)


def finish(adv, sums, adv_hbm, cond_ref, out_sem):
    species = adv_hbm.shape[0]
    outs = [
        pltpu.make_async_copy(adv.at[:, :, s, :], adv_hbm.at[s], out_sem.at[s])
        for s in range(species)
    ]
    for copy in outs:
        copy.start()
    whole = sums[...]
    means = whole / jnp.maximum(whole[ROWS - 1 : ROWS], 1.0)
    for part in range(4):
        cond_ref[:, part, :] = means[0:species, part * NB : (part + 1) * NB]
    for copy in outs:
        copy.wait()


def on_device(comp, diff, temp, weight, jac, bins, pos):
    species, planes, rows, cells = comp.shape
    nx = lax.axis_size("gy") // YLO
    ny = lax.axis_size("sec") * YLO
    per = pos.shape[0] // 2 // lax.axis_size("gx")
    dma = pltpu.SemaphoreType.DMA
    anywhere = pl.BlockSpec(memory_space=pltpu.HBM)
    vmem = pl.BlockSpec(memory_space=pltpu.VMEM)
    adv, sums = pl.pallas_call(
        functools.partial(kernel, species),
        out_shape=(
            pltpu.VMEM((planes, rows, ROWS, cells), F32),
            pltpu.VMEM((ROWS, 4 * NB), F32),
        ),
        in_specs=[anywhere] * 7,
        out_specs=(vmem, vmem),
        scratch_shapes=[
            pltpu.VMEM((planes + 2, rows + 2, ROWS, cells), F32),
            pltpu.VMEM((planes, NB, rows * cells), BF16),
            pltpu.VMEM((2, 5 * NB, cells), BF16),
            pltpu.VMEM((planes, rows, cells), F32),
            pltpu.VMEM((rows, ROWS, cells), F32),
            pltpu.VMEM((planes, rows, cells), F32),
            pltpu.VMEM((planes, rows, cells), jnp.int32),
            pltpu.VMEM(jac.shape, F32),
            pltpu.VMEM((ROWS, ROWS), F32),
            pltpu.SMEM(weight.shape, F32),
            pltpu.SMEM(pos.shape, jnp.int32),
            pltpu.VMEM((planes, ROWS, NB), F32),
            pltpu.VMEM((2, ROWS, cells), F32),
            pltpu.VMEM((2, ROWS, cells), F32),
            pltpu.VMEM((1, nx, 8, 6 * NB), F32),
            pltpu.VMEM((1, ny, 16, 6 * NB), F32),
            pltpu.VMEM((8, 4 * NB), F32),
            pltpu.VMEM((16, 4 * NB), F32),
            pltpu.VMEM((2, ny, 8, 4 * NB), F32),
            pltpu.VMEM((2, nx, 16, 4 * NB), F32),
            dma((29,)),
            dma((6,)),
            dma((6,)),
            dma((1, nx)),
            dma((1, nx)),
            dma((1, ny)),
            dma((1, ny)),
            dma((2, ny)),
            dma((2, ny)),
            dma((2, nx)),
            dma((2, nx)),
            pltpu.SemaphoreType.REGULAR,
        ],
        compiler_params=pltpu.CompilerParams(
            collective_id=0, has_side_effects=True, vmem_limit_bytes=65420000
        ),
        name="section",
    )(comp, diff, temp, weight, jac, bins, pos)
    return pl.pallas_call(
        finish,
        out_shape=(
            jax.ShapeDtypeStruct(comp.shape, F32),
            jax.ShapeDtypeStruct((species, per, NB), F32),
        ),
        in_specs=[vmem, vmem],
        out_specs=(anywhere, vmem),
        scratch_shapes=[dma((species,))],
        compiler_params=pltpu.CompilerParams(vmem_limit_bytes=8 << 20),
        name="finish",
    )(adv, sums)


def solution(mesh):
    in_specs = (
        P(None, "gx", "gy", "sec"),
        P("gx", "gy", "sec"),
        P("gx", "gy", "sec"),
        P(),
        P(),
        P("gx", "gy", "sec"),
        P(),
    )
    out_specs = (P(None, "gx", "gy", "sec"), P(None, "gx", None))
    return jax.shard_map(
        on_device, mesh=mesh, in_specs=in_specs, out_specs=out_specs, check_vma=False
    )
```

```python
import functools

import jax
import jax.numpy as jnp
from jax import lax
from jax.experimental import pallas as pl
from jax.experimental.pallas import tpu as pltpu
from jax.sharding import PartitionSpec as P

NB = 64
YLO = 2
ROWS = 24
F32, BF16 = jnp.float32, jnp.bfloat16
MESH = pl.DeviceIdType.MESH
GROUPS = ((0,), (1, 2), (3, 4), (5, 6), (7,))


def remote(src, dst, send, recv, peer):
    return pltpu.make_async_remote_copy(
        src_ref=src, dst_ref=dst, send_sem=send, recv_sem=recv, device_id=peer, device_id_type=MESH
    )


def split(values):
    hi = values.astype(BF16).astype(F32)
    return jnp.concatenate([hi, values - hi], axis=0).astype(BF16)


def binned(values, hot):
    both = lax.dot_general(
        split(values), hot, (((1,), (1,)), ((), ())), preferred_element_type=F32
    )
    return both[0:ROWS] + both[ROWS : 2 * ROWS]


def kernel(
    species,
    comp_hbm,
    diff_hbm,
    temp_hbm,
    weight_hbm,
    jac_hbm,
    bins_hbm,
    pos_hbm,
    adv,
    sums,
    u,
    onehot,
    onehot_z,
    rate,
    flux_x,
    flux_z,
    source_a,
    source_b,
    parts_a,
    parts_b,
    temp,
    bins,
    jac,
    jac_pad,
    weight,
    pos,
    psum,
    zsend,
    zrecv,
    r1a,
    r1b,
    next_a,
    next_b,
    r2a,
    r2b,
    in_sem,
    hs_sem,
    hr_sem,
    s1a,
    q1a,
    s1b,
    q1b,
    s2a,
    q2a,
    s2b,
    q2b,
    ready,
):
    nsec, ngx, ngy = lax.axis_size("sec"), lax.axis_size("gx"), lax.axis_size("gy")
    nx, ny = ngy // YLO, nsec * YLO
    sec, gx, gy = lax.axis_index("sec"), lax.axis_index("gx"), lax.axis_index("gy")
    my_x, my_y = lax.rem(gy, nx), sec * YLO + gy // nx
    planes, rows = 8, 16
    dif = species

    def device(s, i, g):
        return {"sec": s, "gx": i, "gy": g}

    def at_xy(i, x, y):
        return device(y // YLO, i, lax.rem(y, YLO) * nx + x)

    right, left = lax.rem(gx + 1, ngx), lax.rem(gx + ngx - 1, ngx)
    front, back = lax.rem(gy + 1, ngy), lax.rem(gy + ngy - 1, ngy)
    up, down = lax.rem(sec + 1, nsec), lax.rem(sec + nsec - 1, nsec)

    loads = [
        pltpu.make_async_copy(comp_hbm.at[s], u.at[1:9, 1:17, s, :], in_sem.at[s])
        for s in range(species)
    ]
    loads.append(pltpu.make_async_copy(diff_hbm, u.at[1:9, 1:17, dif, :], in_sem.at[species]))
    first = [
        pltpu.make_async_copy(bins_hbm, bins, in_sem.at[24]),
        pltpu.make_async_copy(temp_hbm, temp, in_sem.at[25]),
        pltpu.make_async_copy(jac_hbm, jac, in_sem.at[26]),
        pltpu.make_async_copy(weight_hbm, weight, in_sem.at[27]),
        pltpu.make_async_copy(pos_hbm, pos, in_sem.at[28]),
    ]
    barrier = pltpu.get_barrier_semaphore()
    inner_left, inner_right = gx > 0, gx < ngx - 1
    peers = [
        device(sec, left, gy),
        device(sec, gx, front),
        device(sec, gx, back),
        device(up, gx, gy),
        device(down, gx, gy),
        at_xy(gx, lax.rem(my_x + 1, nx), my_y),
        at_xy(gx, lax.rem(my_x + nx - 1, nx), my_y),
        at_xy(gx, my_x, lax.rem(my_y + 1, ny)),
        at_xy(gx, my_x, lax.rem(my_y + ny - 1, ny)),
    ]

    @pl.when(inner_right)
    def _():
        pl.semaphore_signal(
            barrier, inc=1, device_id=device(sec, right, gy), device_id_type=MESH
        )

    for peer in peers:
        pl.semaphore_signal(barrier, inc=1, device_id=peer, device_id_type=MESH)
    for copy in first[0:2] + loads + first[2:]:
        copy.start()

    ones = jnp.ones((1, 128), F32)
    level = lax.broadcasted_iota(jnp.int32, (NB, 128), 0)
    for copy in first:
        copy.wait()

    def prepare(x, carry):
        for y in range(rows):
            row = bins[x, pl.ds(y, 1), :]
            onehot[x, :, y * 128 : (y + 1) * 128] = jnp.where(
                jnp.broadcast_to(row, (NB, 128)) == level, 1.0, 0.0
            ).astype(BF16)
            u[x + 1, y + 1, dif + 1 : dif + 2, :] = ones
        rate[x] = 0.2 * jnp.exp(-2.0 / temp[x])
        return carry

    lax.fori_loop(0, planes, prepare, 0)
    flux_x[...] = jnp.zeros_like(flux_x)
    jac_pad[...] = jnp.zeros_like(jac_pad)
    jac_pad[0:species, 0:species] = jac[...]
    j_full = jac_pad[...]
    j_hi = j_full.astype(BF16).astype(F32)
    j_lo = j_full - j_hi
    j_all = jnp.concatenate([j_hi, j_hi, j_lo, j_lo], axis=1).astype(BF16)
    row_id = lax.broadcasted_iota(jnp.int32, (ROWS, 128), 0)
    lane_id = lax.broadcasted_iota(jnp.int32, (ROWS, 128), 1)
    wk = jnp.zeros((ROWS, 128), F32)
    for s in range(species):
        wk = jnp.where(row_id == s, 0.025 * weight[s], wk)

    across = jnp.transpose(bins[...].reshape(planes * rows, 128).astype(F32))
    lane1 = lax.broadcasted_iota(jnp.int32, (1, 128), 1)
    group_of = (lane1 // rows + 1) // 2
    code_level = lax.broadcasted_iota(jnp.int32, (5 * NB, 128), 0)
    for side, lane in ((0, 0), (1, 127)):
        code = across[lane : lane + 1, :].astype(jnp.int32) + group_of * NB
        onehot_z[side] = jnp.where(
            jnp.broadcast_to(code, (5 * NB, 128)) == code_level, 1.0, 0.0
        ).astype(BF16)

    @pl.when(jnp.logical_not(inner_left))
    def _():
        u[0] = jnp.zeros(u.shape[1:], F32)

    @pl.when(jnp.logical_not(inner_right))
    def _():
        u[planes + 1] = jnp.zeros(u.shape[1:], F32)

    for copy in loads:
        copy.wait()
    pl.semaphore_wait(barrier, len(peers) + jnp.minimum(gx, 1))

    halo = [
        remote(u.at[8, 1:17], u.at[0, 1:17], hs_sem.at[0], hr_sem.at[0], device(sec, right, gy)),
        remote(u.at[1, 1:17], u.at[9, 1:17], hs_sem.at[1], hr_sem.at[1], device(sec, left, gy)),
        remote(u.at[1:9, 16], u.at[1:9, 0], hs_sem.at[2], hr_sem.at[2], device(sec, gx, front)),
        remote(u.at[1:9, 1], u.at[1:9, 17], hs_sem.at[3], hr_sem.at[3], device(sec, gx, back)),
        remote(zsend.at[1], zrecv.at[0], hs_sem.at[4], hr_sem.at[4], device(up, gx, gy)),
        remote(zsend.at[0], zrecv.at[1], hs_sem.at[5], hr_sem.at[5], device(down, gx, gy)),
    ]

    @pl.when(inner_right)
    def _():
        halo[0].start()

    @pl.when(inner_left)
    def _():
        halo[1].start()

    for copy in halo[2:4]:
        copy.start()

    packed = []
    for x in range(planes):
        heads = tails = None
        for y in range(rows):
            c = u[x + 1, y + 1]
            turned = pltpu.roll(c, y, 1) if y else c
            heads = turned if y == 0 else jnp.where(lane_id == y, turned, heads)
            tails = turned if y == 0 else jnp.where(lane_id == y - 1, turned, tails)
        packed.append((heads, tails))
    low = high = None
    for x, (heads, tails) in enumerate(packed):
        heads = pltpu.roll(heads, x * rows, 1) if x else heads
        tails = pltpu.roll(tails, x * rows + 1, 1)
        here = lane_id >= x * rows
        low = heads if x == 0 else jnp.where(here, heads, low)
        high = tails if x == 0 else jnp.where(here, tails, high)
    zsend[0] = low
    zsend[1] = high
    for copy in halo[4:6]:
        copy.start()

    inside = lax.broadcasted_iota(jnp.int32, (1, 128), 1) < 127

    def react(x, source):
        parts = split(jnp.concatenate([u[x + 1, y + 1] for y in range(rows)], axis=1))
        source[...] = jnp.dot(
            j_all, jnp.concatenate([parts, parts], axis=0), preferred_element_type=F32
        )

    def advance(x, source, parts):
        xp = jnp.minimum(x + 2, 8)
        for y in range(rows):
            c = u[x + 1, y + 1]
            d = u[x + 1, y + 1, dif : dif + 1, :]
            turned = pltpu.roll(c, 127, 1)
            gain = jnp.where(inside, d + turned[dif : dif + 1], 0.0)
            out = gain * (turned - c)
            flux_z[y] = out - pltpu.roll(out, 1, 1)
        flux_y = None
        for y in range(rows):
            c = u[x + 1, y + 1]
            d = u[x + 1, y + 1, dif : dif + 1, :]
            after = (d + u[xp, y + 1, dif : dif + 1, :]) * (u[xp, y + 1] - c)
            flux = flux_z[y] + (after - flux_x[y])
            flux_x[y] = after
            if y < rows - 1:
                later = (d + u[x + 1, y + 2, dif : dif + 1, :]) * (u[x + 1, y + 2] - c)
                flux = flux + (later if flux_y is None else later - flux_y)
                flux_y = later
            else:
                flux = flux - flux_y
            here = slice(y * 128, (y + 1) * 128)
            value = (c + rate[x, pl.ds(y, 1), :] * source[:, here]) + wk * flux
            adv[x, y] = value
            parts[:, here] = split(value)

    def collect(x, parts):
        both = lax.dot_general(
            parts[...], onehot[x], (((1,), (1,)), ((), ())), preferred_element_type=F32
        )
        psum[x] = both[0:ROWS] + both[ROWS : 2 * ROWS]

    react(0, source_a)

    def inner(x, carry):
        collect(jnp.maximum(x - 1, 0), parts_b)
        advance(x, source_a, parts_b)
        react(jnp.minimum(x + 1, planes - 1), source_a)
        return carry

    lax.fori_loop(0, planes, inner, 0)
    collect(planes - 1, parts_b)

    for copy in halo[2:]:
        copy.wait_recv()

    @pl.when(inner_left)
    def _():
        halo[0].wait_recv()

    @pl.when(inner_right)
    def _():
        halo[1].wait_recv()

    near = [at_xy(gx, lax.rem(my_x + o, nx), my_y) for o in range(1, nx)]
    near += [at_xy(gx, my_x, lax.rem(my_y + o, ny)) for o in range(1, ny)]
    for peer in near:
        pl.semaphore_signal(ready, inc=1, device_id=peer, device_id_type=MESH)

    def face(c, d, other, d_other, gate):
        return wk * ((d + d_other * gate) * (other * gate - c))

    def gate_of(there):
        return jnp.where(there, 1.0, 0.0)

    faces_x = []
    for x, ghost, gate in ((0, 0, 1.0), (7, 9, 1.0)):
        terms = []
        for y in range(rows):
            term = face(
                u[x + 1, y + 1],
                u[x + 1, y + 1, dif : dif + 1, :],
                u[ghost, y + 1],
                u[ghost, y + 1, dif : dif + 1, :],
                gate,
            )
            adv[x, y] = adv[x, y] + term
            terms.append(term)
        faces_x.append(binned(jnp.concatenate(terms, axis=1), onehot[x]))

    gate_back, gate_front = gate_of(gy > 0), gate_of(gy < ngy - 1)
    plane_sums = []
    for x in range(planes):
        terms = []
        for y, ghost, gate in ((0, 0, gate_back), (15, 17, gate_front)):
            term = face(
                u[x + 1, y + 1],
                u[x + 1, y + 1, dif : dif + 1, :],
                u[x + 1, ghost],
                u[x + 1, ghost, dif : dif + 1, :],
                gate,
            )
            adv[x, y] = adv[x, y] + term
            terms.append(term)
        hot = jnp.concatenate([onehot[x, :, 0:128], onehot[x, :, 15 * 128 : 16 * 128]], axis=1)
        total = psum[x] + binned(jnp.concatenate(terms, axis=1), hot)
        if x in (0, 7):
            total = total + faces_x[x // 7]
        plane_sums.append(total)
    ends = []
    for side, gate in ((0, gate_of(sec > 0)), (1, gate_of(sec < nsec - 1))):
        c, other = zsend[side], zrecv[side]
        ends.append(face(c, c[dif : dif + 1], other, other[dif : dif + 1], gate))
    by_group = binned(ends[0], onehot_z[0]) + binned(ends[1], onehot_z[1])

    totals = []
    for g, members in enumerate(GROUPS):
        total = by_group[:, g * NB : (g + 1) * NB]
        for x in members:
            total = total + plane_sums[x]
        totals.append(total)
    totals.append(jnp.zeros_like(totals[0]))
    for k in range(3):
        pair = jnp.concatenate(totals[2 * k : 2 * k + 2], axis=1)
        r1b[0, my_y, :, k * 128 : (k + 1) * 128] = pair[8:24]
        r1a[0, my_x, :, k * 128 : (k + 1) * 128] = pair[0:8]

    waits = []

    def send(src, dst, sem, recv, peer):
        copy = remote(src, dst, sem, recv, peer)
        copy.start()
        waits.append(copy)

    far_y = sorted(range(1, ny), key=lambda o: -min(o, ny - o))
    far_x = sorted(range(1, nx), key=lambda o: -min(o, nx - o))
    for o in far_y:
        block = r1b.at[0, my_y]
        send(block, block, s1b.at[0, o], q1b.at[0, my_y], at_xy(gx, my_x, lax.rem(my_y + o, ny)))
    for o in far_x:
        block = r1a.at[0, my_x]
        send(block, block, s1a.at[0, o], q1a.at[0, my_x], at_xy(gx, lax.rem(my_x + o, nx), my_y))

    def ends_in(x, carry):
        a, b = carry
        a = pltpu.roll(a, lax.rem(128 - x * rows, 128), 1)
        b = pltpu.roll(b, 127 - x * rows, 1)
        for y in range(rows):
            head = pltpu.roll(a, 128 - y, 1) if y else a
            tail = pltpu.roll(b, 128 - y, 1) if y else b
            adv[x, y] = adv[x, y] + jnp.where(
                lane_id == 0, head, jnp.where(lane_id == 127, tail, 0.0)
            )
        return carry

    lax.fori_loop(0, planes, ends_in, (ends[0], ends[1]))

    def arrived(buffer, sem):
        pltpu.make_async_copy(buffer, buffer, sem).wait()

    def gather(buffer, sems, mine, size, layers):
        for o in range(size):
            slot = lax.rem(mine + o, size)
            for layer in range(layers):
                if layer or o:
                    arrived(buffer.at[layer, slot], sems.at[layer, slot])
        total = buffer[0, 0]
        for layer in range(layers):
            for slot in range(size):
                if layer or slot:
                    total = total + buffer[layer, slot]
        return total

    count = pos.shape[0] // 2
    per = count // ngx
    m = lax.rem(pos[gx * planes] - gx * per + count, count)

    def stations(total):
        p = [total[:, k * 128 : (k + 1) * 128] for k in range(3)]
        turned = [pltpu.roll(v, NB, 1) for v in p]
        high = lax.broadcasted_iota(jnp.int32, p[0].shape, 1) >= NB
        q = [jnp.where(high, turned[k], turned[k - 1] if k else 0.0) for k in range(3)]
        flag = [jnp.where(m == k, 1.0, 0.0) for k in range(4)]
        zero = jnp.zeros_like(p[0])
        shifted = (p + [zero], q + [zero], [zero] + p, [zero] + q)
        out = []
        for k in range(4):
            out.append(sum(flag[i] * shifted[i][k] for i in range(4)))
        return jnp.concatenate(out[0:2], axis=1), jnp.concatenate(out[2:4], axis=1)

    own, following = stations(gather(r1a, q1a, my_x, nx, 1))
    r2a[0, my_y] = own
    next_a[...] = following
    pl.semaphore_wait(ready, len(near))
    for o in far_y + [0]:
        peer = lax.rem(my_y + o, ny)
        send(next_a, r2a.at[1, my_y], s2a.at[1, o], q2a.at[1, my_y], at_xy(right, my_x, peer))
        if o:
            block = r2a.at[0, my_y]
            send(block, block, s2a.at[0, o], q2a.at[0, my_y], at_xy(gx, my_x, peer))
    own, following = stations(gather(r1b, q1b, my_y, ny, 1))
    r2b[0, my_x] = own
    next_b[...] = following
    for o in far_x + [0]:
        peer = lax.rem(my_x + o, nx)
        send(next_b, r2b.at[1, my_x], s2b.at[1, o], q2b.at[1, my_x], at_xy(right, peer, my_y))
        if o:
            block = r2b.at[0, my_x]
            send(block, block, s2b.at[0, o], q2b.at[0, my_x], at_xy(gx, peer, my_y))
    for copy in halo[2:] + waits:
        copy.wait_send()

    @pl.when(inner_right)
    def _():
        halo[0].wait_send()

    @pl.when(inner_left)
    def _():
        halo[1].wait_send()

    sums[8:24] = gather(r2b, q2b, my_x, nx, 2)
    sums[0:8] = gather(r2a, q2a, my_y, ny, 2)


def finish(adv, sums, adv_hbm, cond_hbm, cond, out_sem):
    species = adv_hbm.shape[0]
    outs = [
        pltpu.make_async_copy(adv.at[:, :, s, :], adv_hbm.at[s], out_sem.at[s])
        for s in range(species)
    ]
    for copy in outs:
        copy.start()
    whole = sums[...]
    means = whole / jnp.maximum(whole[ROWS - 1 : ROWS], 1.0)
    for part in range(4):
        cond[:, part, :] = means[0:species, part * NB : (part + 1) * NB]
    last = pltpu.make_async_copy(cond, cond_hbm, out_sem.at[species])
    last.start()
    for copy in outs:
        copy.wait()
    last.wait()


def on_device(comp, diff, temp, weight, jac, bins, pos):
    species, planes, rows, cells = comp.shape
    nx = lax.axis_size("gy") // YLO
    ny = lax.axis_size("sec") * YLO
    per = pos.shape[0] // 2 // lax.axis_size("gx")
    dma = pltpu.SemaphoreType.DMA
    anywhere = pl.BlockSpec(memory_space=pltpu.HBM)
    vmem = pl.BlockSpec(memory_space=pltpu.VMEM)
    adv, sums = pl.pallas_call(
        functools.partial(kernel, species),
        out_shape=(
            pltpu.VMEM((planes, rows, ROWS, cells), F32),
            pltpu.VMEM((ROWS, 4 * NB), F32),
        ),
        in_specs=[anywhere] * 7,
        out_specs=(vmem, vmem),
        scratch_shapes=[
            pltpu.VMEM((planes + 2, rows + 2, ROWS, cells), F32),
            pltpu.VMEM((planes, NB, rows * cells), BF16),
            pltpu.VMEM((2, 5 * NB, cells), BF16),
            pltpu.VMEM((planes, rows, cells), F32),
            pltpu.VMEM((rows, ROWS, cells), F32),
            pltpu.VMEM((rows, ROWS, cells), F32),
            pltpu.VMEM((ROWS, rows * cells), F32),
            pltpu.VMEM((ROWS, rows * cells), F32),
            pltpu.VMEM((2 * ROWS, rows * cells), BF16),
            pltpu.VMEM((2 * ROWS, rows * cells), BF16),
            pltpu.VMEM((planes, rows, cells), F32),
            pltpu.VMEM((planes, rows, cells), jnp.int32),
            pltpu.VMEM(jac.shape, F32),
            pltpu.VMEM((ROWS, ROWS), F32),
            pltpu.SMEM(weight.shape, F32),
            pltpu.SMEM(pos.shape, jnp.int32),
            pltpu.VMEM((planes, ROWS, NB), F32),
            pltpu.VMEM((2, ROWS, cells), F32),
            pltpu.VMEM((2, ROWS, cells), F32),
            pltpu.VMEM((1, nx, 8, 6 * NB), F32),
            pltpu.VMEM((1, ny, 16, 6 * NB), F32),
            pltpu.VMEM((8, 4 * NB), F32),
            pltpu.VMEM((16, 4 * NB), F32),
            pltpu.VMEM((2, ny, 8, 4 * NB), F32),
            pltpu.VMEM((2, nx, 16, 4 * NB), F32),
            dma((29,)),
            dma((6,)),
            dma((6,)),
            dma((1, nx)),
            dma((1, nx)),
            dma((1, ny)),
            dma((1, ny)),
            dma((2, ny)),
            dma((2, ny)),
            dma((2, nx)),
            dma((2, nx)),
            pltpu.SemaphoreType.REGULAR,
        ],
        compiler_params=pltpu.CompilerParams(
            collective_id=0, has_side_effects=True, vmem_limit_bytes=65420000
        ),
        name="section",
    )(comp, diff, temp, weight, jac, bins, pos)
    return pl.pallas_call(
        finish,
        out_shape=(
            jax.ShapeDtypeStruct(comp.shape, F32),
            jax.ShapeDtypeStruct((species, per, NB), F32),
        ),
        in_specs=[vmem, vmem],
        out_specs=(anywhere, anywhere),
        scratch_shapes=[pltpu.VMEM((species, per, NB), F32), dma((species + 1,))],
        compiler_params=pltpu.CompilerParams(vmem_limit_bytes=8 << 20),
        name="finish",
    )(adv, sums)


def solution(mesh):
    in_specs = (
        P(None, "gx", "gy", "sec"),
        P("gx", "gy", "sec"),
        P("gx", "gy", "sec"),
        P(),
        P(),
        P("gx", "gy", "sec"),
        P(),
    )
    out_specs = (P(None, "gx", "gy", "sec"), P(None, "gx", None))
    return jax.shard_map(
        on_device, mesh=mesh, in_specs=in_specs, out_specs=out_specs, check_vma=False
    )
```

```python
import functools

import jax
import jax.numpy as jnp
from jax import lax
from jax.experimental import pallas as pl
from jax.experimental.pallas import tpu as pltpu
from jax.sharding import PartitionSpec as P

NB = 64
YLO = 2
ROWS = 24
F32, BF16 = jnp.float32, jnp.bfloat16
MESH = pl.DeviceIdType.MESH
GROUPS = ((0,), (1, 2), (3, 4), (5, 6), (7,))


def remote(src, dst, send, recv, peer):
    return pltpu.make_async_remote_copy(
        src_ref=src, dst_ref=dst, send_sem=send, recv_sem=recv, device_id=peer, device_id_type=MESH
    )


def split(values):
    hi = values.astype(BF16).astype(F32)
    return jnp.concatenate([hi, values - hi], axis=0).astype(BF16)


def binned(values, hot):
    both = lax.dot_general(
        split(values), hot, (((1,), (1,)), ((), ())), preferred_element_type=F32
    )
    return both[0:ROWS] + both[ROWS : 2 * ROWS]


def kernel(
    species,
    comp_hbm,
    diff_hbm,
    temp_hbm,
    weight_hbm,
    jac_hbm,
    bins_hbm,
    pos_hbm,
    adv,
    sums,
    u,
    onehot,
    onehot_z,
    rate,
    flux_x,
    flux_z,
    source_a,
    source_b,
    parts_a,
    parts_b,
    temp,
    bins,
    jac,
    jac_pad,
    weight,
    pos,
    psum,
    zsend,
    zrecv,
    r1a,
    r1b,
    next_a,
    next_b,
    r2a,
    r2b,
    in_sem,
    hs_sem,
    hr_sem,
    s1a,
    q1a,
    s1b,
    q1b,
    s2a,
    q2a,
    s2b,
    q2b,
    ready,
):
    nsec, ngx, ngy = lax.axis_size("sec"), lax.axis_size("gx"), lax.axis_size("gy")
    nx, ny = ngy // YLO, nsec * YLO
    sec, gx, gy = lax.axis_index("sec"), lax.axis_index("gx"), lax.axis_index("gy")
    my_x, my_y = lax.rem(gy, nx), sec * YLO + gy // nx
    planes, rows = 8, 16
    dif = species

    def device(s, i, g):
        return {"sec": s, "gx": i, "gy": g}

    def at_xy(i, x, y):
        return device(y // YLO, i, lax.rem(y, YLO) * nx + x)

    right, left = lax.rem(gx + 1, ngx), lax.rem(gx + ngx - 1, ngx)
    front, back = lax.rem(gy + 1, ngy), lax.rem(gy + ngy - 1, ngy)
    up, down = lax.rem(sec + 1, nsec), lax.rem(sec + nsec - 1, nsec)

    loads = [
        pltpu.make_async_copy(comp_hbm.at[s], u.at[1:9, 1:17, s, :], in_sem.at[s])
        for s in range(species)
    ]
    loads.append(pltpu.make_async_copy(diff_hbm, u.at[1:9, 1:17, dif, :], in_sem.at[species]))
    first = [
        pltpu.make_async_copy(bins_hbm, bins, in_sem.at[24]),
        pltpu.make_async_copy(temp_hbm, temp, in_sem.at[25]),
        pltpu.make_async_copy(jac_hbm, jac, in_sem.at[26]),
        pltpu.make_async_copy(weight_hbm, weight, in_sem.at[27]),
        pltpu.make_async_copy(pos_hbm, pos, in_sem.at[28]),
    ]
    barrier = pltpu.get_barrier_semaphore()
    inner_left, inner_right = gx > 0, gx < ngx - 1
    peers = [
        device(sec, left, gy),
        device(sec, gx, front),
        device(sec, gx, back),
        device(up, gx, gy),
        device(down, gx, gy),
        at_xy(gx, lax.rem(my_x + 1, nx), my_y),
        at_xy(gx, lax.rem(my_x + nx - 1, nx), my_y),
        at_xy(gx, my_x, lax.rem(my_y + 1, ny)),
        at_xy(gx, my_x, lax.rem(my_y + ny - 1, ny)),
    ]

    @pl.when(inner_right)
    def _():
        pl.semaphore_signal(
            barrier, inc=1, device_id=device(sec, right, gy), device_id_type=MESH
        )

    for peer in peers:
        pl.semaphore_signal(barrier, inc=1, device_id=peer, device_id_type=MESH)
    for copy in loads + first:
        copy.start()

    ones = jnp.ones((1, 128), F32)

    def count_row(x, carry):
        for y in range(rows):
            u[x + 1, y + 1, dif + 1 : dif + 2, :] = ones
        return carry

    lax.fori_loop(0, planes, count_row, 0)
    row_id = lax.broadcasted_iota(jnp.int32, (ROWS, 128), 0)
    lane_id = lax.broadcasted_iota(jnp.int32, (ROWS, 128), 1)

    @pl.when(jnp.logical_not(inner_left))
    def _():
        u[0] = jnp.zeros(u.shape[1:], F32)

    @pl.when(jnp.logical_not(inner_right))
    def _():
        u[planes + 1] = jnp.zeros(u.shape[1:], F32)

    for copy in loads:
        copy.wait()
    pl.semaphore_wait(barrier, len(peers) + jnp.minimum(gx, 1))

    halo = [
        remote(u.at[8, 1:17], u.at[0, 1:17], hs_sem.at[0], hr_sem.at[0], device(sec, right, gy)),
        remote(u.at[1, 1:17], u.at[9, 1:17], hs_sem.at[1], hr_sem.at[1], device(sec, left, gy)),
        remote(u.at[1:9, 16], u.at[1:9, 0], hs_sem.at[2], hr_sem.at[2], device(sec, gx, front)),
        remote(u.at[1:9, 1], u.at[1:9, 17], hs_sem.at[3], hr_sem.at[3], device(sec, gx, back)),
        remote(zsend.at[1], zrecv.at[0], hs_sem.at[4], hr_sem.at[4], device(up, gx, gy)),
        remote(zsend.at[0], zrecv.at[1], hs_sem.at[5], hr_sem.at[5], device(down, gx, gy)),
    ]

    @pl.when(inner_right)
    def _():
        halo[0].start()

    @pl.when(inner_left)
    def _():
        halo[1].start()

    for copy in halo[2:4]:
        copy.start()

    packed = []
    for x in range(planes):
        heads = tails = None
        for y in range(rows):
            c = u[x + 1, y + 1]
            turned = pltpu.roll(c, y, 1) if y else c
            heads = turned if y == 0 else jnp.where(lane_id == y, turned, heads)
            tails = turned if y == 0 else jnp.where(lane_id == y - 1, turned, tails)
        packed.append((heads, tails))
    low = high = None
    for x, (heads, tails) in enumerate(packed):
        heads = pltpu.roll(heads, x * rows, 1) if x else heads
        tails = pltpu.roll(tails, x * rows + 1, 1)
        here = lane_id >= x * rows
        low = heads if x == 0 else jnp.where(here, heads, low)
        high = tails if x == 0 else jnp.where(here, tails, high)
    zsend[0] = low
    zsend[1] = high
    for copy in halo[4:6]:
        copy.start()

    level = lax.broadcasted_iota(jnp.int32, (NB, 128), 0)
    for copy in first:
        copy.wait()

    def prepare(x, carry):
        for y in range(rows):
            row = bins[x, pl.ds(y, 1), :]
            onehot[x, :, y * 128 : (y + 1) * 128] = jnp.where(
                jnp.broadcast_to(row, (NB, 128)) == level, 1.0, 0.0
            ).astype(BF16)
        rate[x] = 0.2 * jnp.exp(-2.0 / temp[x])
        return carry

    lax.fori_loop(0, planes, prepare, 0)
    flux_x[...] = jnp.zeros_like(flux_x)
    jac_pad[...] = jnp.zeros_like(jac_pad)
    jac_pad[0:species, 0:species] = jac[...]
    j_full = jac_pad[...]
    j_hi = j_full.astype(BF16).astype(F32)
    j_lo = j_full - j_hi
    j_all = jnp.concatenate([j_hi, j_hi, j_lo, j_lo], axis=1).astype(BF16)
    wk = jnp.zeros((ROWS, 128), F32)
    for s in range(species):
        wk = jnp.where(row_id == s, 0.025 * weight[s], wk)

    across = jnp.transpose(bins[...].reshape(planes * rows, 128).astype(F32))
    lane1 = lax.broadcasted_iota(jnp.int32, (1, 128), 1)
    group_of = (lane1 // rows + 1) // 2
    code_level = lax.broadcasted_iota(jnp.int32, (5 * NB, 128), 0)
    for side, lane in ((0, 0), (1, 127)):
        code = across[lane : lane + 1, :].astype(jnp.int32) + group_of * NB
        onehot_z[side] = jnp.where(
            jnp.broadcast_to(code, (5 * NB, 128)) == code_level, 1.0, 0.0
        ).astype(BF16)

    inside = lax.broadcasted_iota(jnp.int32, (1, 128), 1) < 127

    def react(x, source):
        parts = split(jnp.concatenate([u[x + 1, y + 1] for y in range(rows)], axis=1))
        source[...] = jnp.dot(
            j_all, jnp.concatenate([parts, parts], axis=0), preferred_element_type=F32
        )

    def advance(x, source, parts):
        xp = jnp.minimum(x + 2, 8)
        for y in range(rows):
            c = u[x + 1, y + 1]
            d = u[x + 1, y + 1, dif : dif + 1, :]
            turned = pltpu.roll(c, 127, 1)
            gain = jnp.where(inside, d + turned[dif : dif + 1], 0.0)
            out = gain * (turned - c)
            flux_z[y] = out - pltpu.roll(out, 1, 1)
        flux_y = None
        for y in range(rows):
            c = u[x + 1, y + 1]
            d = u[x + 1, y + 1, dif : dif + 1, :]
            after = (d + u[xp, y + 1, dif : dif + 1, :]) * (u[xp, y + 1] - c)
            flux = flux_z[y] + (after - flux_x[y])
            flux_x[y] = after
            if y < rows - 1:
                later = (d + u[x + 1, y + 2, dif : dif + 1, :]) * (u[x + 1, y + 2] - c)
                flux = flux + (later if flux_y is None else later - flux_y)
                flux_y = later
            else:
                flux = flux - flux_y
            here = slice(y * 128, (y + 1) * 128)
            value = (c + rate[x, pl.ds(y, 1), :] * source[:, here]) + wk * flux
            adv[x, y] = value
            parts[:, here] = split(value)

    def collect(x, parts):
        both = lax.dot_general(
            parts[...], onehot[x], (((1,), (1,)), ((), ())), preferred_element_type=F32
        )
        psum[x] = both[0:ROWS] + both[ROWS : 2 * ROWS]

    react(0, source_a)

    def inner(x, carry):
        collect(jnp.maximum(x - 1, 0), parts_b)
        advance(x, source_a, parts_b)
        react(jnp.minimum(x + 1, planes - 1), source_a)
        return carry

    lax.fori_loop(0, planes, inner, 0)
    collect(planes - 1, parts_b)

    for copy in halo[2:]:
        copy.wait_recv()

    @pl.when(inner_left)
    def _():
        halo[0].wait_recv()

    @pl.when(inner_right)
    def _():
        halo[1].wait_recv()

    near = [at_xy(gx, lax.rem(my_x + o, nx), my_y) for o in range(1, nx)]
    near += [at_xy(gx, my_x, lax.rem(my_y + o, ny)) for o in range(1, ny)]
    for peer in near:
        pl.semaphore_signal(ready, inc=1, device_id=peer, device_id_type=MESH)

    def face(c, d, other, d_other, gate):
        return wk * ((d + d_other * gate) * (other * gate - c))

    def gate_of(there):
        return jnp.where(there, 1.0, 0.0)

    faces_x = []
    for x, ghost, gate in ((0, 0, 1.0), (7, 9, 1.0)):
        terms = []
        for y in range(rows):
            term = face(
                u[x + 1, y + 1],
                u[x + 1, y + 1, dif : dif + 1, :],
                u[ghost, y + 1],
                u[ghost, y + 1, dif : dif + 1, :],
                gate,
            )
            adv[x, y] = adv[x, y] + term
            terms.append(term)
        faces_x.append(binned(jnp.concatenate(terms, axis=1), onehot[x]))

    gate_back, gate_front = gate_of(gy > 0), gate_of(gy < ngy - 1)
    plane_sums = []
    for x in range(planes):
        terms = []
        for y, ghost, gate in ((0, 0, gate_back), (15, 17, gate_front)):
            term = face(
                u[x + 1, y + 1],
                u[x + 1, y + 1, dif : dif + 1, :],
                u[x + 1, ghost],
                u[x + 1, ghost, dif : dif + 1, :],
                gate,
            )
            adv[x, y] = adv[x, y] + term
            terms.append(term)
        hot = jnp.concatenate([onehot[x, :, 0:128], onehot[x, :, 15 * 128 : 16 * 128]], axis=1)
        total = psum[x] + binned(jnp.concatenate(terms, axis=1), hot)
        if x in (0, 7):
            total = total + faces_x[x // 7]
        plane_sums.append(total)
    ends = []
    for side, gate in ((0, gate_of(sec > 0)), (1, gate_of(sec < nsec - 1))):
        c, other = zsend[side], zrecv[side]
        ends.append(face(c, c[dif : dif + 1], other, other[dif : dif + 1], gate))
    by_group = binned(ends[0], onehot_z[0]) + binned(ends[1], onehot_z[1])

    totals = []
    for g, members in enumerate(GROUPS):
        total = by_group[:, g * NB : (g + 1) * NB]
        for x in members:
            total = total + plane_sums[x]
        totals.append(total)
    totals.append(jnp.zeros_like(totals[0]))
    for k in range(3):
        pair = jnp.concatenate(totals[2 * k : 2 * k + 2], axis=1)
        r1b[0, my_y, :, k * 128 : (k + 1) * 128] = pair[8:24]
        r1a[0, my_x, :, k * 128 : (k + 1) * 128] = pair[0:8]

    waits = []

    def send(src, dst, sem, recv, peer):
        copy = remote(src, dst, sem, recv, peer)
        copy.start()
        waits.append(copy)

    far_y = sorted(range(1, ny), key=lambda o: -min(o, ny - o))
    far_x = sorted(range(1, nx), key=lambda o: -min(o, nx - o))
    for o in far_y:
        block = r1b.at[0, my_y]
        send(block, block, s1b.at[0, o], q1b.at[0, my_y], at_xy(gx, my_x, lax.rem(my_y + o, ny)))
    for o in far_x:
        block = r1a.at[0, my_x]
        send(block, block, s1a.at[0, o], q1a.at[0, my_x], at_xy(gx, lax.rem(my_x + o, nx), my_y))

    def ends_in(x, carry):
        a, b = carry
        a = pltpu.roll(a, lax.rem(128 - x * rows, 128), 1)
        b = pltpu.roll(b, 127 - x * rows, 1)
        for y in range(rows):
            head = pltpu.roll(a, 128 - y, 1) if y else a
            tail = pltpu.roll(b, 128 - y, 1) if y else b
            adv[x, y] = adv[x, y] + jnp.where(
                lane_id == 0, head, jnp.where(lane_id == 127, tail, 0.0)
            )
        return carry

    lax.fori_loop(0, planes, ends_in, (ends[0], ends[1]))

    def arrived(buffer, sem):
        pltpu.make_async_copy(buffer, buffer, sem).wait()

    def gather(buffer, sems, mine, size, layers):
        for o in range(size):
            slot = lax.rem(mine + o, size)
            for layer in range(layers):
                if layer or o:
                    arrived(buffer.at[layer, slot], sems.at[layer, slot])
        total = buffer[0, 0]
        for layer in range(layers):
            for slot in range(size):
                if layer or slot:
                    total = total + buffer[layer, slot]
        return total

    count = pos.shape[0] // 2
    per = count // ngx
    m = lax.rem(pos[gx * planes] - gx * per + count, count)

    def stations(total):
        p = [total[:, k * 128 : (k + 1) * 128] for k in range(3)]
        turned = [pltpu.roll(v, NB, 1) for v in p]
        high = lax.broadcasted_iota(jnp.int32, p[0].shape, 1) >= NB
        q = [jnp.where(high, turned[k], turned[k - 1] if k else 0.0) for k in range(3)]
        flag = [jnp.where(m == k, 1.0, 0.0) for k in range(4)]
        zero = jnp.zeros_like(p[0])
        shifted = (p + [zero], q + [zero], [zero] + p, [zero] + q)
        out = []
        for k in range(4):
            out.append(sum(flag[i] * shifted[i][k] for i in range(4)))
        return jnp.concatenate(out[0:2], axis=1), jnp.concatenate(out[2:4], axis=1)

    own, following = stations(gather(r1a, q1a, my_x, nx, 1))
    r2a[0, my_y] = own
    next_a[...] = following
    pl.semaphore_wait(ready, len(near))
    for o in far_y + [0]:
        peer = lax.rem(my_y + o, ny)
        send(next_a, r2a.at[1, my_y], s2a.at[1, o], q2a.at[1, my_y], at_xy(right, my_x, peer))
        if o:
            block = r2a.at[0, my_y]
            send(block, block, s2a.at[0, o], q2a.at[0, my_y], at_xy(gx, my_x, peer))
    own, following = stations(gather(r1b, q1b, my_y, ny, 1))
    r2b[0, my_x] = own
    next_b[...] = following
    for o in far_x + [0]:
        peer = lax.rem(my_x + o, nx)
        send(next_b, r2b.at[1, my_x], s2b.at[1, o], q2b.at[1, my_x], at_xy(right, peer, my_y))
        if o:
            block = r2b.at[0, my_x]
            send(block, block, s2b.at[0, o], q2b.at[0, my_x], at_xy(gx, peer, my_y))
    for copy in halo[2:] + waits:
        copy.wait_send()

    @pl.when(inner_right)
    def _():
        halo[0].wait_send()

    @pl.when(inner_left)
    def _():
        halo[1].wait_send()

    sums[8:24] = gather(r2b, q2b, my_x, nx, 2)
    sums[0:8] = gather(r2a, q2a, my_y, ny, 2)


def finish(adv, sums, adv_hbm, cond_hbm, cond, out_sem):
    species = adv_hbm.shape[0]
    outs = [
        pltpu.make_async_copy(adv.at[:, :, s, :], adv_hbm.at[s], out_sem.at[s])
        for s in range(species)
    ]
    for copy in outs:
        copy.start()
    whole = sums[...]
    means = whole / jnp.maximum(whole[ROWS - 1 : ROWS], 1.0)
    for part in range(4):
        cond[:, part, :] = means[0:species, part * NB : (part + 1) * NB]
    last = pltpu.make_async_copy(cond, cond_hbm, out_sem.at[species])
    last.start()
    for copy in outs:
        copy.wait()
    last.wait()


def on_device(comp, diff, temp, weight, jac, bins, pos):
    species, planes, rows, cells = comp.shape
    nx = lax.axis_size("gy") // YLO
    ny = lax.axis_size("sec") * YLO
    per = pos.shape[0] // 2 // lax.axis_size("gx")
    dma = pltpu.SemaphoreType.DMA
    anywhere = pl.BlockSpec(memory_space=pltpu.HBM)
    vmem = pl.BlockSpec(memory_space=pltpu.VMEM)
    adv, sums = pl.pallas_call(
        functools.partial(kernel, species),
        out_shape=(
            pltpu.VMEM((planes, rows, ROWS, cells), F32),
            pltpu.VMEM((ROWS, 4 * NB), F32),
        ),
        in_specs=[anywhere] * 7,
        out_specs=(vmem, vmem),
        scratch_shapes=[
            pltpu.VMEM((planes + 2, rows + 2, ROWS, cells), F32),
            pltpu.VMEM((planes, NB, rows * cells), BF16),
            pltpu.VMEM((2, 5 * NB, cells), BF16),
            pltpu.VMEM((planes, rows, cells), F32),
            pltpu.VMEM((rows, ROWS, cells), F32),
            pltpu.VMEM((rows, ROWS, cells), F32),
            pltpu.VMEM((ROWS, rows * cells), F32),
            pltpu.VMEM((ROWS, rows * cells), F32),
            pltpu.VMEM((2 * ROWS, rows * cells), BF16),
            pltpu.VMEM((2 * ROWS, rows * cells), BF16),
            pltpu.VMEM((planes, rows, cells), F32),
            pltpu.VMEM((planes, rows, cells), jnp.int32),
            pltpu.VMEM(jac.shape, F32),
            pltpu.VMEM((ROWS, ROWS), F32),
            pltpu.SMEM(weight.shape, F32),
            pltpu.SMEM(pos.shape, jnp.int32),
            pltpu.VMEM((planes, ROWS, NB), F32),
            pltpu.VMEM((2, ROWS, cells), F32),
            pltpu.VMEM((2, ROWS, cells), F32),
            pltpu.VMEM((1, nx, 8, 6 * NB), F32),
            pltpu.VMEM((1, ny, 16, 6 * NB), F32),
            pltpu.VMEM((8, 4 * NB), F32),
            pltpu.VMEM((16, 4 * NB), F32),
            pltpu.VMEM((2, ny, 8, 4 * NB), F32),
            pltpu.VMEM((2, nx, 16, 4 * NB), F32),
            dma((29,)),
            dma((6,)),
            dma((6,)),
            dma((1, nx)),
            dma((1, nx)),
            dma((1, ny)),
            dma((1, ny)),
            dma((2, ny)),
            dma((2, ny)),
            dma((2, nx)),
            dma((2, nx)),
            pltpu.SemaphoreType.REGULAR,
        ],
        compiler_params=pltpu.CompilerParams(
            collective_id=0, has_side_effects=True, vmem_limit_bytes=65420000
        ),
        name="section",
    )(comp, diff, temp, weight, jac, bins, pos)
    return pl.pallas_call(
        finish,
        out_shape=(
            jax.ShapeDtypeStruct(comp.shape, F32),
            jax.ShapeDtypeStruct((species, per, NB), F32),
        ),
        in_specs=[vmem, vmem],
        out_specs=(anywhere, anywhere),
        scratch_shapes=[pltpu.VMEM((species, per, NB), F32), dma((species + 1,))],
        compiler_params=pltpu.CompilerParams(vmem_limit_bytes=8 << 20),
        name="finish",
    )(adv, sums)


def solution(mesh):
    in_specs = (
        P(None, "gx", "gy", "sec"),
        P("gx", "gy", "sec"),
        P("gx", "gy", "sec"),
        P(),
        P(),
        P("gx", "gy", "sec"),
        P(),
    )
    out_specs = (P(None, "gx", "gy", "sec"), P(None, "gx", None))
    return jax.shard_map(
        on_device, mesh=mesh, in_specs=in_specs, out_specs=out_specs, check_vma=False
    )
```

```python
import functools

import jax
import jax.numpy as jnp
from jax import lax
from jax.experimental import pallas as pl
from jax.experimental.pallas import tpu as pltpu
from jax.sharding import PartitionSpec as P

NB = 64
YLO = 2
ROWS = 24
F32, BF16 = jnp.float32, jnp.bfloat16
MESH = pl.DeviceIdType.MESH
GROUPS = ((0,), (1, 2), (3, 4), (5, 6), (7,))


def remote(src, dst, send, recv, peer):
    return pltpu.make_async_remote_copy(
        src_ref=src, dst_ref=dst, send_sem=send, recv_sem=recv, device_id=peer, device_id_type=MESH
    )


def split(values):
    hi = values.astype(BF16).astype(F32)
    return jnp.concatenate([hi, values - hi], axis=0).astype(BF16)


def binned(values, hot):
    both = lax.dot_general(
        split(values), hot, (((1,), (1,)), ((), ())), preferred_element_type=F32
    )
    return both[0:ROWS] + both[ROWS : 2 * ROWS]


def kernel(
    species,
    comp_hbm,
    diff_hbm,
    temp_hbm,
    weight_hbm,
    jac_hbm,
    bins_hbm,
    pos_hbm,
    adv,
    sums,
    u,
    onehot,
    onehot_z,
    rate,
    flux_x,
    flux_z,
    source_a,
    source_b,
    parts_a,
    parts_b,
    temp,
    bins,
    jac,
    jac_pad,
    weight,
    pos,
    psum,
    zsend,
    zrecv,
    r1a,
    r1b,
    next_a,
    next_b,
    r2a,
    r2b,
    in_sem,
    hs_sem,
    hr_sem,
    s1a,
    q1a,
    s1b,
    q1b,
    s2a,
    q2a,
    s2b,
    q2b,
    ready,
):
    nsec, ngx, ngy = lax.axis_size("sec"), lax.axis_size("gx"), lax.axis_size("gy")
    nx, ny = ngy // YLO, nsec * YLO
    sec, gx, gy = lax.axis_index("sec"), lax.axis_index("gx"), lax.axis_index("gy")
    my_x, my_y = lax.rem(gy, nx), sec * YLO + gy // nx
    planes, rows = 8, 16
    dif = species

    def device(s, i, g):
        return {"sec": s, "gx": i, "gy": g}

    def at_xy(i, x, y):
        return device(y // YLO, i, lax.rem(y, YLO) * nx + x)

    right, left = lax.rem(gx + 1, ngx), lax.rem(gx + ngx - 1, ngx)
    front, back = lax.rem(gy + 1, ngy), lax.rem(gy + ngy - 1, ngy)
    up, down = lax.rem(sec + 1, nsec), lax.rem(sec + nsec - 1, nsec)

    loads = [
        pltpu.make_async_copy(comp_hbm.at[s], u.at[1:9, 1:17, s, :], in_sem.at[s])
        for s in range(species)
    ]
    loads.append(pltpu.make_async_copy(diff_hbm, u.at[1:9, 1:17, dif, :], in_sem.at[species]))
    first = [
        pltpu.make_async_copy(bins_hbm, bins, in_sem.at[24]),
        pltpu.make_async_copy(temp_hbm, temp, in_sem.at[25]),
        pltpu.make_async_copy(jac_hbm, jac, in_sem.at[26]),
        pltpu.make_async_copy(weight_hbm, weight, in_sem.at[27]),
        pltpu.make_async_copy(pos_hbm, pos, in_sem.at[28]),
    ]
    barrier = pltpu.get_barrier_semaphore()
    inner_left, inner_right = gx > 0, gx < ngx - 1
    peers = [
        device(sec, left, gy),
        device(sec, gx, front),
        device(sec, gx, back),
        device(up, gx, gy),
        device(down, gx, gy),
        at_xy(gx, my_x, lax.rem(my_y + 1, ny)),
        at_xy(gx, my_x, lax.rem(my_y + ny - 1, ny)),
    ]
    along_x = [at_xy(gx, lax.rem(my_x + o, nx), my_y) for o in range(1, nx)]
    peers += along_x

    @pl.when(inner_right)
    def _():
        pl.semaphore_signal(
            barrier, inc=1, device_id=device(sec, right, gy), device_id_type=MESH
        )

    for peer in peers:
        pl.semaphore_signal(barrier, inc=1, device_id=peer, device_id_type=MESH)
    for copy in first[0:2] + loads + first[2:]:
        copy.start()

    ones = jnp.ones((1, 128), F32)
    level = lax.broadcasted_iota(jnp.int32, (NB, 128), 0)
    for copy in first:
        copy.wait()

    def prepare(x, carry):
        for y in range(rows):
            row = bins[x, pl.ds(y, 1), :]
            onehot[x, :, y * 128 : (y + 1) * 128] = jnp.where(
                jnp.broadcast_to(row, (NB, 128)) == level, 1.0, 0.0
            ).astype(BF16)
            u[x + 1, y + 1, dif + 1 : dif + 2, :] = ones
        rate[x] = 0.2 * jnp.exp(-2.0 / temp[x])
        return carry

    lax.fori_loop(0, planes, prepare, 0)
    flux_x[...] = jnp.zeros_like(flux_x)
    jac_pad[...] = jnp.zeros_like(jac_pad)
    jac_pad[0:species, 0:species] = jac[...]
    j_full = jac_pad[...]
    j_hi = j_full.astype(BF16).astype(F32)
    j_lo = j_full - j_hi
    j_all = jnp.concatenate([j_hi, j_hi, j_lo, j_lo], axis=1).astype(BF16)
    row_id = lax.broadcasted_iota(jnp.int32, (ROWS, 128), 0)
    lane_id = lax.broadcasted_iota(jnp.int32, (ROWS, 128), 1)
    wk = jnp.zeros((ROWS, 128), F32)
    for s in range(species):
        wk = jnp.where(row_id == s, 0.025 * weight[s], wk)

    across = jnp.transpose(bins[...].reshape(planes * rows, 128).astype(F32))
    lane1 = lax.broadcasted_iota(jnp.int32, (1, 128), 1)
    group_of = (lane1 // rows + 1) // 2
    code_level = lax.broadcasted_iota(jnp.int32, (5 * NB, 128), 0)
    for side, lane in ((0, 0), (1, 127)):
        code = across[lane : lane + 1, :].astype(jnp.int32) + group_of * NB
        onehot_z[side] = jnp.where(
            jnp.broadcast_to(code, (5 * NB, 128)) == code_level, 1.0, 0.0
        ).astype(BF16)

    @pl.when(jnp.logical_not(inner_left))
    def _():
        u[0] = jnp.zeros(u.shape[1:], F32)

    @pl.when(jnp.logical_not(inner_right))
    def _():
        u[planes + 1] = jnp.zeros(u.shape[1:], F32)

    for copy in loads:
        copy.wait()
    pl.semaphore_wait(barrier, len(peers) + jnp.minimum(gx, 1))

    halo = [
        remote(u.at[8, 1:17], u.at[0, 1:17], hs_sem.at[0], hr_sem.at[0], device(sec, right, gy)),
        remote(u.at[1, 1:17], u.at[9, 1:17], hs_sem.at[1], hr_sem.at[1], device(sec, left, gy)),
        remote(u.at[1:9, 16], u.at[1:9, 0], hs_sem.at[2], hr_sem.at[2], device(sec, gx, front)),
        remote(u.at[1:9, 1], u.at[1:9, 17], hs_sem.at[3], hr_sem.at[3], device(sec, gx, back)),
        remote(zsend.at[1], zrecv.at[0], hs_sem.at[4], hr_sem.at[4], device(up, gx, gy)),
        remote(zsend.at[0], zrecv.at[1], hs_sem.at[5], hr_sem.at[5], device(down, gx, gy)),
    ]

    @pl.when(inner_right)
    def _():
        halo[0].start()

    @pl.when(inner_left)
    def _():
        halo[1].start()

    for copy in halo[2:4]:
        copy.start()
    for peer in along_x:
        pl.semaphore_signal(ready, inc=1, device_id=peer, device_id_type=MESH)

    packed = []
    for x in range(planes):
        heads = tails = None
        for y in range(rows):
            c = u[x + 1, y + 1]
            turned = pltpu.roll(c, y, 1) if y else c
            heads = turned if y == 0 else jnp.where(lane_id == y, turned, heads)
            tails = turned if y == 0 else jnp.where(lane_id == y - 1, turned, tails)
        packed.append((heads, tails))
    low = high = None
    for x, (heads, tails) in enumerate(packed):
        heads = pltpu.roll(heads, x * rows, 1) if x else heads
        tails = pltpu.roll(tails, x * rows + 1, 1)
        here = lane_id >= x * rows
        low = heads if x == 0 else jnp.where(here, heads, low)
        high = tails if x == 0 else jnp.where(here, tails, high)
    zsend[0] = low
    zsend[1] = high
    for copy in halo[4:6]:
        copy.start()

    inside = lax.broadcasted_iota(jnp.int32, (1, 128), 1) < 127

    def react(x, source):
        parts = split(jnp.concatenate([u[x + 1, y + 1] for y in range(rows)], axis=1))
        source[...] = jnp.dot(
            j_all, jnp.concatenate([parts, parts], axis=0), preferred_element_type=F32
        )

    def advance(x, source, parts):
        xp = jnp.minimum(x + 2, 8)
        for y in range(rows):
            c = u[x + 1, y + 1]
            d = u[x + 1, y + 1, dif : dif + 1, :]
            turned = pltpu.roll(c, 127, 1)
            gain = jnp.where(inside, d + turned[dif : dif + 1], 0.0)
            out = gain * (turned - c)
            flux_z[y] = out - pltpu.roll(out, 1, 1)
        flux_y = None
        for y in range(rows):
            c = u[x + 1, y + 1]
            d = u[x + 1, y + 1, dif : dif + 1, :]
            after = (d + u[xp, y + 1, dif : dif + 1, :]) * (u[xp, y + 1] - c)
            flux = flux_z[y] + (after - flux_x[y])
            flux_x[y] = after
            if y < rows - 1:
                later = (d + u[x + 1, y + 2, dif : dif + 1, :]) * (u[x + 1, y + 2] - c)
                flux = flux + (later if flux_y is None else later - flux_y)
                flux_y = later
            else:
                flux = flux - flux_y
            here = slice(y * 128, (y + 1) * 128)
            value = (c + rate[x, pl.ds(y, 1), :] * source[:, here]) + wk * flux
            adv[x, y] = value
            parts[:, here] = split(value)

    def collect(x, parts):
        both = lax.dot_general(
            parts[...], onehot[x], (((1,), (1,)), ((), ())), preferred_element_type=F32
        )
        psum[x] = both[0:ROWS] + both[ROWS : 2 * ROWS]

    react(0, source_a)

    def inner(x, carry):
        collect(jnp.maximum(x - 1, 0), parts_b)
        advance(x, source_a, parts_b)
        react(jnp.minimum(x + 1, planes - 1), source_a)
        return carry

    lax.fori_loop(0, planes, inner, 0)
    collect(planes - 1, parts_b)

    for copy in halo[2:]:
        copy.wait_recv()

    @pl.when(inner_left)
    def _():
        halo[0].wait_recv()

    @pl.when(inner_right)
    def _():
        halo[1].wait_recv()

    def face(c, d, other, d_other, gate):
        return wk * ((d + d_other * gate) * (other * gate - c))

    def gate_of(there):
        return jnp.where(there, 1.0, 0.0)

    faces_x = []
    for x, ghost, gate in ((0, 0, 1.0), (7, 9, 1.0)):
        terms = []
        for y in range(rows):
            term = face(
                u[x + 1, y + 1],
                u[x + 1, y + 1, dif : dif + 1, :],
                u[ghost, y + 1],
                u[ghost, y + 1, dif : dif + 1, :],
                gate,
            )
            adv[x, y] = adv[x, y] + term
            terms.append(term)
        faces_x.append(binned(jnp.concatenate(terms, axis=1), onehot[x]))

    gate_back, gate_front = gate_of(gy > 0), gate_of(gy < ngy - 1)
    plane_sums = []
    for x in range(planes):
        terms = []
        for y, ghost, gate in ((0, 0, gate_back), (15, 17, gate_front)):
            term = face(
                u[x + 1, y + 1],
                u[x + 1, y + 1, dif : dif + 1, :],
                u[x + 1, ghost],
                u[x + 1, ghost, dif : dif + 1, :],
                gate,
            )
            adv[x, y] = adv[x, y] + term
            terms.append(term)
        hot = jnp.concatenate([onehot[x, :, 0:128], onehot[x, :, 15 * 128 : 16 * 128]], axis=1)
        total = psum[x] + binned(jnp.concatenate(terms, axis=1), hot)
        if x in (0, 7):
            total = total + faces_x[x // 7]
        plane_sums.append(total)
    ends = []
    for side, gate in ((0, gate_of(sec > 0)), (1, gate_of(sec < nsec - 1))):
        c, other = zsend[side], zrecv[side]
        ends.append(face(c, c[dif : dif + 1], other, other[dif : dif + 1], gate))
    by_group = binned(ends[0], onehot_z[0]) + binned(ends[1], onehot_z[1])

    totals = []
    for g, members in enumerate(GROUPS):
        total = by_group[:, g * NB : (g + 1) * NB]
        for x in members:
            total = total + plane_sums[x]
        totals.append(total)
    totals.append(jnp.zeros_like(totals[0]))
    count = pos.shape[0] // 2
    per = count // ngx
    m = lax.rem(pos[gx * planes] - gx * per + count, count)

    def stations(total):
        p = [total[:, k * 128 : (k + 1) * 128] for k in range(3)]
        turned = [pltpu.roll(v, NB, 1) for v in p]
        high = lax.broadcasted_iota(jnp.int32, p[0].shape, 1) >= NB
        q = [jnp.where(high, turned[k], turned[k - 1] if k else 0.0) for k in range(3)]
        flag = [jnp.where(m == k, 1.0, 0.0) for k in range(4)]
        zero = jnp.zeros_like(p[0])
        shifted = (p + [zero], q + [zero], [zero] + p, [zero] + q)
        out = []
        for k in range(4):
            out.append(sum(flag[i] * shifted[i][k] for i in range(4)))
        return jnp.concatenate(out[0:2], axis=1), jnp.concatenate(out[2:4], axis=1)

    grouped = jnp.concatenate(totals, axis=1)
    own, following = stations(grouped[8:24])
    r1b[0, my_y] = grouped[0:8]
    r1a[0, my_x] = own
    next_a[...] = following

    waits = []

    def send(src, dst, sem, recv, peer):
        copy = remote(src, dst, sem, recv, peer)
        copy.start()
        waits.append(copy)

    far_y = sorted(range(1, ny), key=lambda o: -min(o, ny - o))
    far_x = sorted(range(1, nx), key=lambda o: -min(o, nx - o))

    def along_y(block, send_sem, recv_sem):
        for o in far_y:
            peer = at_xy(gx, my_x, lax.rem(my_y + o, ny))
            send(block, block, send_sem.at[0, o], recv_sem.at[0, my_y], peer)

    def over_x(buffer, following, send_sem, recv_sem):
        block = buffer.at[0, my_x]
        for o in far_x + [0]:
            x = lax.rem(my_x + o, nx)
            peer = at_xy(right, x, my_y)
            send(following, buffer.at[1, my_x], send_sem.at[1, o], recv_sem.at[1, my_x], peer)
            if o:
                peer = at_xy(gx, x, my_y)
                send(block, block, send_sem.at[0, o], recv_sem.at[0, my_x], peer)

    along_y(r1b.at[0, my_y], s1b, q1b)
    pl.semaphore_wait(ready, len(along_x))
    over_x(r1a, next_a, s1a, q1a)

    def ends_in(x, carry):
        a, b = carry
        a = pltpu.roll(a, lax.rem(128 - x * rows, 128), 1)
        b = pltpu.roll(b, 127 - x * rows, 1)
        for y in range(rows):
            head = pltpu.roll(a, 128 - y, 1) if y else a
            tail = pltpu.roll(b, 128 - y, 1) if y else b
            adv[x, y] = adv[x, y] + jnp.where(
                lane_id == 0, head, jnp.where(lane_id == 127, tail, 0.0)
            )
        return carry

    lax.fori_loop(0, planes, ends_in, (ends[0], ends[1]))

    def arrived(buffer, sem):
        pltpu.make_async_copy(buffer, buffer, sem).wait()

    def gather(buffer, sems, mine, size, layers):
        for o in range(size):
            slot = lax.rem(mine + o, size)
            for layer in range(layers):
                if layer or o:
                    arrived(buffer.at[layer, slot], sems.at[layer, slot])
        total = buffer[0, 0]
        for layer in range(layers):
            for slot in range(size):
                if layer or slot:
                    total = total + buffer[layer, slot]
        return total

    r2a[0, my_y] = gather(r1a, q1a, my_x, nx, 2)
    along_y(r2a.at[0, my_y], s2a, q2a)
    own, following = stations(gather(r1b, q1b, my_y, ny, 1))
    r2b[0, my_x] = own
    next_b[...] = following
    over_x(r2b, next_b, s2b, q2b)
    for copy in halo[2:] + waits:
        copy.wait_send()

    @pl.when(inner_right)
    def _():
        halo[0].wait_send()

    @pl.when(inner_left)
    def _():
        halo[1].wait_send()

    sums[0:8] = gather(r2b, q2b, my_x, nx, 2)
    sums[8:24] = gather(r2a, q2a, my_y, ny, 1)


def finish(adv, sums, adv_hbm, cond_hbm, cond, out_sem):
    species = adv_hbm.shape[0]
    outs = [
        pltpu.make_async_copy(adv.at[:, :, s, :], adv_hbm.at[s], out_sem.at[s])
        for s in range(species)
    ]
    for copy in outs:
        copy.start()
    whole = sums[...]
    means = whole / jnp.maximum(whole[ROWS - 1 : ROWS], 1.0)
    for part in range(4):
        cond[:, part, :] = means[0:species, part * NB : (part + 1) * NB]
    last = pltpu.make_async_copy(cond, cond_hbm, out_sem.at[species])
    last.start()
    for copy in outs:
        copy.wait()
    last.wait()


def on_device(comp, diff, temp, weight, jac, bins, pos):
    species, planes, rows, cells = comp.shape
    nx = lax.axis_size("gy") // YLO
    ny = lax.axis_size("sec") * YLO
    per = pos.shape[0] // 2 // lax.axis_size("gx")
    dma = pltpu.SemaphoreType.DMA
    anywhere = pl.BlockSpec(memory_space=pltpu.HBM)
    vmem = pl.BlockSpec(memory_space=pltpu.VMEM)
    adv, sums = pl.pallas_call(
        functools.partial(kernel, species),
        out_shape=(
            pltpu.VMEM((planes, rows, ROWS, cells), F32),
            pltpu.VMEM((ROWS, 4 * NB), F32),
        ),
        in_specs=[anywhere] * 7,
        out_specs=(vmem, vmem),
        scratch_shapes=[
            pltpu.VMEM((planes + 2, rows + 2, ROWS, cells), F32),
            pltpu.VMEM((planes, NB, rows * cells), BF16),
            pltpu.VMEM((2, 5 * NB, cells), BF16),
            pltpu.VMEM((planes, rows, cells), F32),
            pltpu.VMEM((rows, ROWS, cells), F32),
            pltpu.VMEM((rows, ROWS, cells), F32),
            pltpu.VMEM((ROWS, rows * cells), F32),
            pltpu.VMEM((ROWS, rows * cells), F32),
            pltpu.VMEM((2 * ROWS, rows * cells), BF16),
            pltpu.VMEM((2 * ROWS, rows * cells), BF16),
            pltpu.VMEM((planes, rows, cells), F32),
            pltpu.VMEM((planes, rows, cells), jnp.int32),
            pltpu.VMEM(jac.shape, F32),
            pltpu.VMEM((ROWS, ROWS), F32),
            pltpu.SMEM(weight.shape, F32),
            pltpu.SMEM(pos.shape, jnp.int32),
            pltpu.VMEM((planes, ROWS, NB), F32),
            pltpu.VMEM((2, ROWS, cells), F32),
            pltpu.VMEM((2, ROWS, cells), F32),
            pltpu.VMEM((2, nx, 16, 4 * NB), F32),
            pltpu.VMEM((1, ny, 8, 6 * NB), F32),
            pltpu.VMEM((16, 4 * NB), F32),
            pltpu.VMEM((8, 4 * NB), F32),
            pltpu.VMEM((1, ny, 16, 4 * NB), F32),
            pltpu.VMEM((2, nx, 8, 4 * NB), F32),
            dma((29,)),
            dma((6,)),
            dma((6,)),
            dma((2, nx)),
            dma((2, nx)),
            dma((1, ny)),
            dma((1, ny)),
            dma((1, ny)),
            dma((1, ny)),
            dma((2, nx)),
            dma((2, nx)),
            pltpu.SemaphoreType.REGULAR,
        ],
        compiler_params=pltpu.CompilerParams(
            collective_id=0, has_side_effects=True, vmem_limit_bytes=65420000
        ),
        name="section",
    )(comp, diff, temp, weight, jac, bins, pos)
    return pl.pallas_call(
        finish,
        out_shape=(
            jax.ShapeDtypeStruct(comp.shape, F32),
            jax.ShapeDtypeStruct((species, per, NB), F32),
        ),
        in_specs=[vmem, vmem],
        out_specs=(anywhere, anywhere),
        scratch_shapes=[pltpu.VMEM((species, per, NB), F32), dma((species + 1,))],
        compiler_params=pltpu.CompilerParams(vmem_limit_bytes=8 << 20),
        name="finish",
    )(adv, sums)


def solution(mesh):
    in_specs = (
        P(None, "gx", "gy", "sec"),
        P("gx", "gy", "sec"),
        P("gx", "gy", "sec"),
        P(),
        P(),
        P("gx", "gy", "sec"),
        P(),
    )
    out_specs = (P(None, "gx", "gy", "sec"), P(None, "gx", None))
    return jax.shard_map(
        on_device, mesh=mesh, in_specs=in_specs, out_specs=out_specs, check_vma=False
    )
```

```python
import functools

import jax
import jax.numpy as jnp
from jax import lax
from jax.experimental import pallas as pl
from jax.experimental.pallas import tpu as pltpu
from jax.sharding import PartitionSpec as P

NB = 64
YLO = 2
ROWS = 24
F32, BF16 = jnp.float32, jnp.bfloat16
MESH = pl.DeviceIdType.MESH
GROUPS = ((0,), (1, 2), (3, 4), (5, 6), (7,))


def remote(src, dst, send, recv, peer):
    return pltpu.make_async_remote_copy(
        src_ref=src, dst_ref=dst, send_sem=send, recv_sem=recv, device_id=peer, device_id_type=MESH
    )


def split(values):
    hi = values.astype(BF16).astype(F32)
    return jnp.concatenate([hi, values - hi], axis=0).astype(BF16)


def binned(values, hot):
    both = lax.dot_general(
        split(values), hot, (((1,), (1,)), ((), ())), preferred_element_type=F32
    )
    return both[0:ROWS] + both[ROWS : 2 * ROWS]


def kernel(
    species,
    comp_hbm,
    diff_hbm,
    temp_hbm,
    weight_hbm,
    jac_hbm,
    bins_hbm,
    pos_hbm,
    adv,
    sums,
    u,
    onehot,
    onehot_z,
    rate,
    flux_x,
    flux_z,
    source_a,
    source_b,
    parts_a,
    parts_b,
    temp,
    bins,
    jac,
    jac_pad,
    weight,
    pos,
    psum,
    zsend,
    zrecv,
    r1a,
    r1b,
    next_a,
    next_b,
    r2a,
    r2b,
    in_sem,
    hs_sem,
    hr_sem,
    s1a,
    q1a,
    s1b,
    q1b,
    s2a,
    q2a,
    s2b,
    q2b,
    ready,
):
    nsec, ngx, ngy = lax.axis_size("sec"), lax.axis_size("gx"), lax.axis_size("gy")
    nx, ny = ngy // YLO, nsec * YLO
    sec, gx, gy = lax.axis_index("sec"), lax.axis_index("gx"), lax.axis_index("gy")
    my_x, my_y = lax.rem(gy, nx), sec * YLO + gy // nx
    planes, rows = 8, 16
    dif = species

    def device(s, i, g):
        return {"sec": s, "gx": i, "gy": g}

    def at_xy(i, x, y):
        return device(y // YLO, i, lax.rem(y, YLO) * nx + x)

    right, left = lax.rem(gx + 1, ngx), lax.rem(gx + ngx - 1, ngx)
    front, back = lax.rem(gy + 1, ngy), lax.rem(gy + ngy - 1, ngy)
    up, down = lax.rem(sec + 1, nsec), lax.rem(sec + nsec - 1, nsec)

    loads = [
        pltpu.make_async_copy(comp_hbm.at[s], u.at[1:9, 1:17, s, :], in_sem.at[s])
        for s in range(species)
    ]
    loads.append(pltpu.make_async_copy(diff_hbm, u.at[1:9, 1:17, dif, :], in_sem.at[species]))
    first = [
        pltpu.make_async_copy(bins_hbm, bins, in_sem.at[24]),
        pltpu.make_async_copy(temp_hbm, temp, in_sem.at[25]),
        pltpu.make_async_copy(jac_hbm, jac, in_sem.at[26]),
        pltpu.make_async_copy(weight_hbm, weight, in_sem.at[27]),
        pltpu.make_async_copy(pos_hbm, pos, in_sem.at[28]),
    ]
    barrier = pltpu.get_barrier_semaphore()
    inner_left, inner_right = gx > 0, gx < ngx - 1
    peers = [
        device(sec, left, gy),
        device(sec, gx, front),
        device(sec, gx, back),
        device(up, gx, gy),
        device(down, gx, gy),
        at_xy(gx, my_x, lax.rem(my_y + 1, ny)),
        at_xy(gx, my_x, lax.rem(my_y + ny - 1, ny)),
    ]
    along_x = [at_xy(gx, lax.rem(my_x + o, nx), my_y) for o in range(1, nx)]
    peers += along_x

    @pl.when(inner_right)
    def _():
        pl.semaphore_signal(
            barrier, inc=1, device_id=device(sec, right, gy), device_id_type=MESH
        )

    for peer in peers:
        pl.semaphore_signal(barrier, inc=1, device_id=peer, device_id_type=MESH)
    for copy in first[0:2] + loads + first[2:]:
        copy.start()

    ones = jnp.ones((1, 128), F32)
    level = lax.broadcasted_iota(jnp.int32, (NB, 128), 0)
    for copy in first:
        copy.wait()

    def prepare(x, carry):
        for y in range(rows):
            row = bins[x, pl.ds(y, 1), :]
            onehot[x, :, y * 128 : (y + 1) * 128] = jnp.where(
                jnp.broadcast_to(row, (NB, 128)) == level, 1.0, 0.0
            ).astype(BF16)
            u[x + 1, y + 1, dif + 1 : dif + 2, :] = ones
        rate[x] = 0.2 * jnp.exp(-2.0 / temp[x])
        return carry

    lax.fori_loop(0, planes, prepare, 0)
    flux_x[...] = jnp.zeros_like(flux_x)
    jac_pad[...] = jnp.zeros_like(jac_pad)
    jac_pad[0:species, 0:species] = jac[...]
    j_full = jac_pad[...]
    j_hi = j_full.astype(BF16).astype(F32)
    j_lo = j_full - j_hi
    j_all = jnp.concatenate([j_hi, j_hi, j_lo, j_lo], axis=1).astype(BF16)
    row_id = lax.broadcasted_iota(jnp.int32, (ROWS, 128), 0)
    lane_id = lax.broadcasted_iota(jnp.int32, (ROWS, 128), 1)
    wk = jnp.zeros((ROWS, 128), F32)
    for s in range(species):
        wk = jnp.where(row_id == s, 0.025 * weight[s], wk)

    across = jnp.transpose(bins[...].reshape(planes * rows, 128).astype(F32))
    lane1 = lax.broadcasted_iota(jnp.int32, (1, 128), 1)
    group_of = (lane1 // rows + 1) // 2
    code_level = lax.broadcasted_iota(jnp.int32, (5 * NB, 128), 0)
    for side, lane in ((0, 0), (1, 127)):
        code = across[lane : lane + 1, :].astype(jnp.int32) + group_of * NB
        onehot_z[side] = jnp.where(
            jnp.broadcast_to(code, (5 * NB, 128)) == code_level, 1.0, 0.0
        ).astype(BF16)

    @pl.when(jnp.logical_not(inner_left))
    def _():
        u[0] = jnp.zeros(u.shape[1:], F32)

    @pl.when(jnp.logical_not(inner_right))
    def _():
        u[planes + 1] = jnp.zeros(u.shape[1:], F32)

    for copy in loads:
        copy.wait()
    pl.semaphore_wait(barrier, len(peers) + jnp.minimum(gx, 1))

    halo = [
        remote(u.at[8, 1:17], u.at[0, 1:17], hs_sem.at[0], hr_sem.at[0], device(sec, right, gy)),
        remote(u.at[1, 1:17], u.at[9, 1:17], hs_sem.at[1], hr_sem.at[1], device(sec, left, gy)),
        remote(u.at[1:9, 16], u.at[1:9, 0], hs_sem.at[2], hr_sem.at[2], device(sec, gx, front)),
        remote(u.at[1:9, 1], u.at[1:9, 17], hs_sem.at[3], hr_sem.at[3], device(sec, gx, back)),
        remote(zsend.at[1], zrecv.at[0], hs_sem.at[4], hr_sem.at[4], device(up, gx, gy)),
        remote(zsend.at[0], zrecv.at[1], hs_sem.at[5], hr_sem.at[5], device(down, gx, gy)),
    ]

    @pl.when(inner_right)
    def _():
        halo[0].start()

    @pl.when(inner_left)
    def _():
        halo[1].start()

    for copy in halo[2:4]:
        copy.start()
    for peer in along_x:
        pl.semaphore_signal(ready, inc=1, device_id=peer, device_id_type=MESH)

    packed = []
    for x in range(planes):
        heads = tails = None
        for y in range(rows):
            c = u[x + 1, y + 1]
            turned = pltpu.roll(c, y, 1) if y else c
            heads = turned if y == 0 else jnp.where(lane_id == y, turned, heads)
            tails = turned if y == 0 else jnp.where(lane_id == y - 1, turned, tails)
        packed.append((heads, tails))
    low = high = None
    for x, (heads, tails) in enumerate(packed):
        heads = pltpu.roll(heads, x * rows, 1) if x else heads
        tails = pltpu.roll(tails, x * rows + 1, 1)
        here = lane_id >= x * rows
        low = heads if x == 0 else jnp.where(here, heads, low)
        high = tails if x == 0 else jnp.where(here, tails, high)
    zsend[0] = low
    zsend[1] = high
    for copy in halo[4:6]:
        copy.start()

    inside = lax.broadcasted_iota(jnp.int32, (1, 128), 1) < 127

    def react(x, source):
        parts = split(jnp.concatenate([u[x + 1, y + 1] for y in range(rows)], axis=1))
        source[...] = jnp.dot(
            j_all, jnp.concatenate([parts, parts], axis=0), preferred_element_type=F32
        )

    def advance(x, source, parts):
        xp = jnp.minimum(x + 2, 8)
        for y in range(rows):
            c = u[x + 1, y + 1]
            d = u[x + 1, y + 1, dif : dif + 1, :]
            turned = pltpu.roll(c, 127, 1)
            gain = jnp.where(inside, d + turned[dif : dif + 1], 0.0)
            out = gain * (turned - c)
            flux_z[y] = out - pltpu.roll(out, 1, 1)
        flux_y = None
        for y in range(rows):
            c = u[x + 1, y + 1]
            d = u[x + 1, y + 1, dif : dif + 1, :]
            after = (d + u[xp, y + 1, dif : dif + 1, :]) * (u[xp, y + 1] - c)
            flux = flux_z[y] + (after - flux_x[y])
            flux_x[y] = after
            if y < rows - 1:
                later = (d + u[x + 1, y + 2, dif : dif + 1, :]) * (u[x + 1, y + 2] - c)
                flux = flux + (later if flux_y is None else later - flux_y)
                flux_y = later
            else:
                flux = flux - flux_y
            here = slice(y * 128, (y + 1) * 128)
            value = (c + rate[x, pl.ds(y, 1), :] * source[:, here]) + wk * flux
            adv[x, y] = value
            parts[:, here] = split(value)

    def collect(x, parts):
        both = lax.dot_general(
            parts[...], onehot[x], (((1,), (1,)), ((), ())), preferred_element_type=F32
        )
        psum[x] = both[0:ROWS] + both[ROWS : 2 * ROWS]

    react(0, source_a)

    def inner(x, carry):
        collect(jnp.maximum(x - 1, 0), parts_b)
        advance(x, source_a, parts_b)
        react(jnp.minimum(x + 1, planes - 1), source_a)
        return carry

    lax.fori_loop(0, planes, inner, 0)
    collect(planes - 1, parts_b)

    for copy in halo[4:6]:
        copy.wait_recv()

    def face(c, d, other, d_other, gate):
        return wk * ((d + d_other * gate) * (other * gate - c))

    def gate_of(there):
        return jnp.where(there, 1.0, 0.0)

    ends = []
    for side, gate in ((0, gate_of(sec > 0)), (1, gate_of(sec < nsec - 1))):
        c, other = zsend[side], zrecv[side]
        ends.append(face(c, c[dif : dif + 1], other, other[dif : dif + 1], gate))
    by_group = binned(ends[0], onehot_z[0]) + binned(ends[1], onehot_z[1])

    for copy in halo[2:4]:
        copy.wait_recv()
    gate_back, gate_front = gate_of(gy > 0), gate_of(gy < ngy - 1)
    plane_sums = []
    for x in range(planes):
        terms = []
        for y, ghost, gate in ((0, 0, gate_back), (15, 17, gate_front)):
            term = face(
                u[x + 1, y + 1],
                u[x + 1, y + 1, dif : dif + 1, :],
                u[x + 1, ghost],
                u[x + 1, ghost, dif : dif + 1, :],
                gate,
            )
            adv[x, y] = adv[x, y] + term
            terms.append(term)
        hot = jnp.concatenate([onehot[x, :, 0:128], onehot[x, :, 15 * 128 : 16 * 128]], axis=1)
        total = psum[x] + binned(jnp.concatenate(terms, axis=1), hot)
        plane_sums.append(total)

    @pl.when(inner_left)
    def _():
        halo[0].wait_recv()

    @pl.when(inner_right)
    def _():
        halo[1].wait_recv()

    faces_x = []
    for x, ghost, gate in ((0, 0, 1.0), (7, 9, 1.0)):
        terms = []
        for y in range(rows):
            term = face(
                u[x + 1, y + 1],
                u[x + 1, y + 1, dif : dif + 1, :],
                u[ghost, y + 1],
                u[ghost, y + 1, dif : dif + 1, :],
                gate,
            )
            adv[x, y] = adv[x, y] + term
            terms.append(term)
        faces_x.append(binned(jnp.concatenate(terms, axis=1), onehot[x]))
    plane_sums[0] = plane_sums[0] + faces_x[0]
    plane_sums[7] = plane_sums[7] + faces_x[1]
    totals = []
    for g, members in enumerate(GROUPS):
        total = by_group[:, g * NB : (g + 1) * NB]
        for x in members:
            total = total + plane_sums[x]
        totals.append(total)
    totals.append(jnp.zeros_like(totals[0]))
    count = pos.shape[0] // 2
    per = count // ngx
    m = lax.rem(pos[gx * planes] - gx * per + count, count)

    def stations(total):
        p = [total[:, k * 128 : (k + 1) * 128] for k in range(3)]
        turned = [pltpu.roll(v, NB, 1) for v in p]
        high = lax.broadcasted_iota(jnp.int32, p[0].shape, 1) >= NB
        q = [jnp.where(high, turned[k], turned[k - 1] if k else 0.0) for k in range(3)]
        flag = [jnp.where(m == k, 1.0, 0.0) for k in range(4)]
        zero = jnp.zeros_like(p[0])
        shifted = (p + [zero], q + [zero], [zero] + p, [zero] + q)
        out = []
        for k in range(4):
            out.append(sum(flag[i] * shifted[i][k] for i in range(4)))
        return jnp.concatenate(out[0:2], axis=1), jnp.concatenate(out[2:4], axis=1)

    grouped = jnp.concatenate(totals, axis=1)
    own, following = stations(grouped[8:24])
    r1b[0, my_y] = grouped[0:8]
    r1a[0, my_x] = own
    next_a[...] = following

    waits = []

    def send(src, dst, sem, recv, peer):
        copy = remote(src, dst, sem, recv, peer)
        copy.start()
        waits.append(copy)

    far_y = sorted(range(1, ny), key=lambda o: -min(o, ny - o))
    far_x = sorted(range(1, nx), key=lambda o: -min(o, nx - o))

    def along_y(block, send_sem, recv_sem):
        for o in far_y:
            peer = at_xy(gx, my_x, lax.rem(my_y + o, ny))
            send(block, block, send_sem.at[0, o], recv_sem.at[0, my_y], peer)

    def over_x(buffer, following, send_sem, recv_sem):
        block = buffer.at[0, my_x]
        for o in far_x + [0]:
            x = lax.rem(my_x + o, nx)
            peer = at_xy(right, x, my_y)
            send(following, buffer.at[1, my_x], send_sem.at[1, o], recv_sem.at[1, my_x], peer)
            if o:
                peer = at_xy(gx, x, my_y)
                send(block, block, send_sem.at[0, o], recv_sem.at[0, my_x], peer)

    pl.semaphore_wait(ready, len(along_x))
    over_x(r1a, next_a, s1a, q1a)
    along_y(r1b.at[0, my_y], s1b, q1b)

    def ends_in(x, carry):
        a, b = carry
        a = pltpu.roll(a, lax.rem(128 - x * rows, 128), 1)
        b = pltpu.roll(b, 127 - x * rows, 1)
        for y in range(rows):
            head = pltpu.roll(a, 128 - y, 1) if y else a
            tail = pltpu.roll(b, 128 - y, 1) if y else b
            adv[x, y] = adv[x, y] + jnp.where(
                lane_id == 0, head, jnp.where(lane_id == 127, tail, 0.0)
            )
        return carry

    lax.fori_loop(0, planes, ends_in, (ends[0], ends[1]))

    def arrived(buffer, sem):
        pltpu.make_async_copy(buffer, buffer, sem).wait()

    def gather(buffer, sems, mine, size, layers):
        for o in range(size):
            slot = lax.rem(mine + o, size)
            for layer in range(layers):
                if layer or o:
                    arrived(buffer.at[layer, slot], sems.at[layer, slot])
        total = buffer[0, 0]
        for layer in range(layers):
            for slot in range(size):
                if layer or slot:
                    total = total + buffer[layer, slot]
        return total

    r2a[0, my_y] = gather(r1a, q1a, my_x, nx, 2)
    along_y(r2a.at[0, my_y], s2a, q2a)
    own, following = stations(gather(r1b, q1b, my_y, ny, 1))
    r2b[0, my_x] = own
    next_b[...] = following
    over_x(r2b, next_b, s2b, q2b)
    for copy in halo[2:] + waits:
        copy.wait_send()

    @pl.when(inner_right)
    def _():
        halo[0].wait_send()

    @pl.when(inner_left)
    def _():
        halo[1].wait_send()

    sums[0:8] = gather(r2b, q2b, my_x, nx, 2)
    sums[8:24] = gather(r2a, q2a, my_y, ny, 1)


def finish(adv, sums, adv_hbm, cond_hbm, cond, out_sem):
    species = adv_hbm.shape[0]
    outs = [
        pltpu.make_async_copy(adv.at[:, :, s, :], adv_hbm.at[s], out_sem.at[s])
        for s in range(species)
    ]
    for copy in outs:
        copy.start()
    whole = sums[...]
    means = whole / jnp.maximum(whole[ROWS - 1 : ROWS], 1.0)
    for part in range(4):
        cond[:, part, :] = means[0:species, part * NB : (part + 1) * NB]
    last = pltpu.make_async_copy(cond, cond_hbm, out_sem.at[species])
    last.start()
    for copy in outs:
        copy.wait()
    last.wait()


def on_device(comp, diff, temp, weight, jac, bins, pos):
    species, planes, rows, cells = comp.shape
    nx = lax.axis_size("gy") // YLO
    ny = lax.axis_size("sec") * YLO
    per = pos.shape[0] // 2 // lax.axis_size("gx")
    dma = pltpu.SemaphoreType.DMA
    anywhere = pl.BlockSpec(memory_space=pltpu.HBM)
    vmem = pl.BlockSpec(memory_space=pltpu.VMEM)
    adv, sums = pl.pallas_call(
        functools.partial(kernel, species),
        out_shape=(
            pltpu.VMEM((planes, rows, ROWS, cells), F32),
            pltpu.VMEM((ROWS, 4 * NB), F32),
        ),
        in_specs=[anywhere] * 7,
        out_specs=(vmem, vmem),
        scratch_shapes=[
            pltpu.VMEM((planes + 2, rows + 2, ROWS, cells), F32),
            pltpu.VMEM((planes, NB, rows * cells), BF16),
            pltpu.VMEM((2, 5 * NB, cells), BF16),
            pltpu.VMEM((planes, rows, cells), F32),
            pltpu.VMEM((rows, ROWS, cells), F32),
            pltpu.VMEM((rows, ROWS, cells), F32),
            pltpu.VMEM((ROWS, rows * cells), F32),
            pltpu.VMEM((ROWS, rows * cells), F32),
            pltpu.VMEM((2 * ROWS, rows * cells), BF16),
            pltpu.VMEM((2 * ROWS, rows * cells), BF16),
            pltpu.VMEM((planes, rows, cells), F32),
            pltpu.VMEM((planes, rows, cells), jnp.int32),
            pltpu.VMEM(jac.shape, F32),
            pltpu.VMEM((ROWS, ROWS), F32),
            pltpu.SMEM(weight.shape, F32),
            pltpu.SMEM(pos.shape, jnp.int32),
            pltpu.VMEM((planes, ROWS, NB), F32),
            pltpu.VMEM((2, ROWS, cells), F32),
            pltpu.VMEM((2, ROWS, cells), F32),
            pltpu.VMEM((2, nx, 16, 4 * NB), F32),
            pltpu.VMEM((1, ny, 8, 6 * NB), F32),
            pltpu.VMEM((16, 4 * NB), F32),
            pltpu.VMEM((8, 4 * NB), F32),
            pltpu.VMEM((1, ny, 16, 4 * NB), F32),
            pltpu.VMEM((2, nx, 8, 4 * NB), F32),
            dma((29,)),
            dma((6,)),
            dma((6,)),
            dma((2, nx)),
            dma((2, nx)),
            dma((1, ny)),
            dma((1, ny)),
            dma((1, ny)),
            dma((1, ny)),
            dma((2, nx)),
            dma((2, nx)),
            pltpu.SemaphoreType.REGULAR,
        ],
        compiler_params=pltpu.CompilerParams(
            collective_id=0, has_side_effects=True, vmem_limit_bytes=65420000
        ),
        name="section",
    )(comp, diff, temp, weight, jac, bins, pos)
    return pl.pallas_call(
        finish,
        out_shape=(
            jax.ShapeDtypeStruct(comp.shape, F32),
            jax.ShapeDtypeStruct((species, per, NB), F32),
        ),
        in_specs=[vmem, vmem],
        out_specs=(anywhere, anywhere),
        scratch_shapes=[pltpu.VMEM((species, per, NB), F32), dma((species + 1,))],
        compiler_params=pltpu.CompilerParams(vmem_limit_bytes=8 << 20),
        name="finish",
    )(adv, sums)


def solution(mesh):
    in_specs = (
        P(None, "gx", "gy", "sec"),
        P("gx", "gy", "sec"),
        P("gx", "gy", "sec"),
        P(),
        P(),
        P("gx", "gy", "sec"),
        P(),
    )
    out_specs = (P(None, "gx", "gy", "sec"), P(None, "gx", None))
    return jax.shard_map(
        on_device, mesh=mesh, in_specs=in_specs, out_specs=out_specs, check_vma=False
    )
```
